512 devices in a mesh: state: 64 (over y_hi, z, core), basis: 8 (over y_lo, x).
Axes of the slice: x: 4, y: 8 (y_hi: 4, y_lo: 2; y = y_hi * 2 + y_lo), z: 8, core: 2. Of those that a mesh axis runs over, the one named last changes fastest.
Arguments:
- upper_coef: bfloat16 [24576, 16384], P('basis', 'state'), may hold values from -6 to 6
- lower_state_store: bfloat16 [24576, 8192], P('basis', 'state'), may hold values from -0.0390625 to 0.0390625
- owners: int32 [4], replicated, may hold values from 0 to 63, as said below
- dipole: bfloat16 [192, 3, 128, 128], P('basis'), may hold values from -0.3125 to 0.3125
- offsets: int32 [192, 3], P('basis'), may hold values from -2 to 2
- lower_energy: float32 [512], P('basis'), may hold values from 0 to 2
- upper_energy: float32 [16384], P('state'), may hold values from 2.5 to 5
Outputs:
- moments: float32 [512, 16384], P('basis', 'state')
- intensity: float32 [512, 16384], P('basis', 'state')
The draws below stay inside these ranges and needn't reach their ends.
Inputs may be any that keep to these rules, and one draw needn't show every extreme that they name: owners are distinct state indices.
All inputs are finite; a program needn't handle non-finite values.
Results may differ from the reference program's by a relative error of at most 0.009.
Values may be sent and summed in bfloat16 or wider, within the bound.
No kernel may reach another device: no remote copies, remote signals or barrier semaphores. Data moves between devices by JAX's collectives and lax.ppermute only.
A program may use at most 128 MiB of HBM per device.

```python
import jax
import jax.numpy as jnp
from jax import lax

BS = 128
COLUMN_BLOCKS = 3
REACH = 2
PANEL = 128
PANELS = 4
NBLK = 192
NB = 24576
UPPER = 16384
LOWER = 512
POOL = 8192
N_STATE = 64


def draw_owners(key, part):
    first = jax.random.fold_in(key, 11)
    second = jax.random.fold_in(key, 23)
    others = jax.random.permutation(first, N_STATE - 1)[:PANELS - 1].astype(jnp.int32)
    listed = jnp.concatenate([others, jnp.full((1,), N_STATE - 1, jnp.int32)])
    order = jax.random.permutation(second, PANELS)
    return listed[order].astype(jnp.int32)


def with_ends(entries, stream_key, low, top_value):
    shape = entries.shape
    place = [jax.random.randint(jax.random.fold_in(stream_key, axis), (), 0, shape[axis]) for axis in range(len(shape))]
    entries = entries.at[tuple(place)].set(low)
    longest = shape.index(max(shape))
    place[longest] = (place[longest] + 1) % shape[longest]
    return entries.at[tuple(place)].set(top_value)


def levels(stream_key, dims, split, least, largest):
    def one(position, parts):
        draws = jax.random.uniform(jax.random.fold_in(jax.random.fold_in(stream_key, 6), position), (parts,), jnp.float32, least / len(split), largest / len(split))
        return jnp.repeat(jnp.exp(draws), dims[position] // parts).reshape((-1,) + (1,) * (len(dims) - position - 1))

    gain = one(*split[0])
    for cut in split[1:]:
        gain = gain * one(*cut)
    return gain


def noise(rng, dims, deviation, most, cuts=(), kind=jnp.bfloat16):
    array = deviation * jax.random.normal(rng, dims, jnp.float32)
    if cuts:
        array = array * levels(rng, dims, cuts, -0.22, 0.18)
    return jnp.clip(array, -most, most).astype(kind)


def setup_inputs(seed: int = 0) -> dict:
    streams_of = jax.random.split(jax.random.key(seed), 8)
    return {
        "upper_coef": noise(streams_of[0], (NB, UPPER), 1.0, 6.0, ((0, 8), (1, 64))),
        "lower_state_store": noise(streams_of[1], (NB, POOL), NB ** -0.5, 0.0390625, ((0, 8), (1, 64))),
        "owners": draw_owners(jax.random.fold_in(streams_of[7], 71), 0),
        "dipole": noise(streams_of[3], (NBLK, COLUMN_BLOCKS, BS, BS), (COLUMN_BLOCKS * BS) ** -0.5, 0.3125, ((0, 8),)),
        "offsets": with_ends(jax.random.randint(streams_of[4], (NBLK, COLUMN_BLOCKS), 0 - REACH, REACH + 1), jax.random.fold_in(streams_of[4], 1), 0 - REACH, REACH).astype(jnp.int32),
        "lower_energy": jnp.clip(2.0 * jax.random.uniform(streams_of[5], (LOWER,), jnp.float32) ** levels(streams_of[5], (LOWER,), ((0, 8),), -0.2, 0.2), 0.0, 2.0),
        "upper_energy": jnp.clip(2.5 + 2.5 * jax.random.uniform(streams_of[6], (UPPER,), jnp.float32) ** levels(streams_of[6], (UPPER,), ((0, 64),), -0.2, 0.2), 2.5, 5.0),
    }


def reference(upper_coef, lower_state_store, owners, dipole, offsets, lower_energy, upper_energy):
    pieces = [lax.dynamic_slice_in_dim(lower_state_store, (owners[p] * PANEL).astype(jnp.int32), PANEL, 1) for p in range(PANELS)]
    panels = jnp.concatenate(pieces, axis=1)
    padded = jnp.pad(panels, ((REACH * BS, REACH * BS), (0, 0)))
    coef_blocks = upper_coef.reshape(NBLK, BS, UPPER)
    block_ids = jnp.arange(NBLK, dtype=jnp.int32)

    def step(total, xs):
        blocks, offs, coef, col = xs
        half = jnp.zeros((LOWER, BS), jnp.float32)
        for k in range(COLUMN_BLOCKS):
            start = ((col + offs[k] + REACH) * BS).astype(jnp.int32)
            rows = lax.dynamic_slice_in_dim(padded, start, BS, 0)
            half = half + jnp.dot(rows.T, blocks[k], preferred_element_type=jnp.float32)
        half_low = half.astype(jnp.bfloat16)
        total = total + jnp.dot(half_low, coef, preferred_element_type=jnp.float32)
        return total, None

    moments, _ = lax.scan(step, jnp.zeros((LOWER, UPPER), jnp.float32), (dipole, offsets, coef_blocks, block_ids))
    nu = upper_energy[None, :] - lower_energy[:, None]
    intensity = moments * moments * nu * jnp.exp(-lower_energy)[:, None] * (1.0 - jnp.exp(-nu))
    return moments, intensity
```

```python
import jax
import jax.numpy as jnp
from jax import lax
from jax.sharding import Mesh
from jax.sharding import PartitionSpec as P

BS = 128
REACH = 2
PANELS = 4
BF16 = jnp.bfloat16
F32 = jnp.float32

SIZES = {"yhi": 4, "z": 8, "core": 2, "ylo": 2, "x": 4}
STATE = ("yhi", "z", "core")
BASIS = ("ylo", "x")
GATHER_ORDER = ("core", "z", "yhi")


def own_half(store, dipole, offsets):
    nblk = dipole.shape[0]
    count = lax.axis_size(BASIS)
    width = REACH * BS
    up = lax.ppermute(store[-width:], BASIS, [(i, i + 1) for i in range(count - 1)])
    down = lax.ppermute(store[:width], BASIS, [(i + 1, i) for i in range(count - 1)])
    blocked = jnp.concatenate([up, store, down], axis=0).reshape(nblk + 2 * REACH, BS, -1)
    rows = jnp.arange(nblk, dtype=jnp.int32)[:, None] + offsets + REACH
    picked = blocked[rows]
    half = jnp.einsum("ckdz,ckdq->czq", dipole, picked, preferred_element_type=F32)
    return half.astype(BF16).reshape(store.shape)


def on_device(upper_coef, store, owners, dipole, offsets, lower_energy, upper_energy):
    half = own_half(store, dipole, offsets)
    pieces = lax.all_to_all(half, GATHER_ORDER, 0, 0, tiled=True)
    members = lax.axis_size(GATHER_ORDER)
    pieces = pieces.reshape(members, -1, half.shape[1])
    core = owners % 2
    z = (owners // 2) % SIZES["z"]
    yhi = owners // (2 * SIZES["z"])
    source = (core * SIZES["z"] + z) * SIZES["yhi"] + yhi
    chunk = jnp.concatenate(
        [lax.dynamic_index_in_dim(pieces, source[p], 0, keepdims=False) for p in range(PANELS)],
        axis=1,
    )
    chunk = lax.all_gather(chunk, "yhi", axis=0, tiled=True)
    chunk = lax.all_gather(chunk, "z", axis=0, tiled=True)
    other = lax.ppermute(chunk, "core", [(0, 1), (1, 0)])
    first = lax.axis_index("core") == 0
    rows = chunk.shape[0]
    mine = lax.axis_index("core") * rows
    theirs = rows - mine
    dims = (((0,), (0,)), ((), ()))
    share = lax.dot_general(
        chunk, lax.dynamic_slice_in_dim(upper_coef, mine, rows, 0), dims, preferred_element_type=F32
    ) + lax.dot_general(
        other, lax.dynamic_slice_in_dim(upper_coef, theirs, rows, 0), dims, preferred_element_type=F32
    )
    shares = lax.all_to_all(share.astype(BF16), BASIS, 0, 0, tiled=True)
    shares = shares.reshape(lax.axis_size(BASIS), -1, share.shape[1])
    moments = jnp.sum(shares.astype(F32), axis=0)
    nu = upper_energy[None, :] - lower_energy[:, None]
    intensity = moments * moments * nu * jnp.exp(-lower_energy)[:, None] * (1.0 - jnp.exp(-nu))
    return moments, intensity


def solution(mesh):
    fine = Mesh(mesh.devices.reshape(tuple(SIZES.values())), tuple(SIZES))
    placed = (
        P(BASIS, STATE),
        P(BASIS, STATE),
        P(),
        P(BASIS, None, None, None),
        P(BASIS, None),
        P(BASIS),
        P(STATE),
    )
    return jax.shard_map(
        on_device,
        mesh=fine,
        in_specs=placed,
        out_specs=(P(BASIS, STATE), P(BASIS, STATE)),
        check_vma=False,
    )
```

```python
import jax
import jax.numpy as jnp
from jax import lax
from jax.sharding import Mesh
from jax.sharding import PartitionSpec as P

BS = 128
REACH = 2
PANELS = 4
BF16 = jnp.bfloat16
F32 = jnp.float32

SIZES = {"yhi": 4, "z": 8, "core": 2, "ylo": 2, "x": 4}
STATE = ("yhi", "z", "core")
BASIS = ("ylo", "x")
CHIPS = ("z", "yhi")


def chip_half(store, dipole, offsets, core):
    rows, width = store.shape
    ncol = dipole.shape[0] // 2
    reach = REACH * BS
    inside = rows // 2 + reach
    count = lax.axis_size(BASIS)
    swap = [(0, 1), (1, 0)]

    def member(basis, kind):
        return basis + count * kind

    own_pairs = [(member(b, 0), member(b + 1, 0)) for b in range(count - 1)]
    own_pairs += [(member(b + 1, 1), member(b, 1)) for b in range(count - 1)]
    other_pairs = [(member(b, 1), member(b + 1, 0)) for b in range(count - 1)]
    other_pairs += [(member(b + 1, 0), member(b, 1)) for b in range(count - 1)]
    span = rows - reach
    axes = ("core",) + BASIS
    own_edge = lax.ppermute(
        lax.dynamic_slice_in_dim(store, (1 - core) * span, reach, 0), axes, own_pairs
    )
    other_edge = lax.ppermute(
        lax.dynamic_slice_in_dim(store, core * span, reach, 0), axes, other_pairs
    )
    step = rows - inside
    other = lax.ppermute(
        lax.dynamic_slice_in_dim(store, (1 - core) * step, inside, 0), "core", swap
    )
    own = lax.dynamic_slice_in_dim(store, core * step, inside, 0)
    near = jnp.concatenate(
        [jnp.concatenate([own, other], 1), jnp.concatenate([own_edge, other_edge], 1)], 0
    )
    blocks = near.reshape(-1, BS, 2 * width)
    nblocks = blocks.shape[0]
    local_dipole = lax.dynamic_slice_in_dim(dipole, core * ncol, ncol, 0)
    local_offsets = lax.dynamic_slice_in_dim(offsets, core * ncol, ncol, 0)
    place = jnp.arange(ncol, dtype=jnp.int32)[:, None] + local_offsets + core * REACH
    picked = blocks[place % nblocks]
    half = jnp.einsum("ckdz,ckdq->czq", local_dipole, picked, preferred_element_type=F32)
    return half.astype(BF16).reshape(ncol * BS, 2 * width)


def on_device(upper_coef, store, owners, dipole, offsets, lower_energy, upper_energy):
    core = lax.axis_index("core")
    width = store.shape[1]
    half = chip_half(store, dipole, offsets, core)
    chips = lax.axis_size(CHIPS)
    rows = half.shape[0]

    pieces = lax.all_to_all(half, CHIPS, 0, 0, tiled=True)
    pieces = pieces.reshape(chips, rows // chips, 2 * width)

    sent = lax.dynamic_slice_in_dim(upper_coef, (1 - core) * rows, rows, 0)
    kept = lax.dynamic_slice_in_dim(upper_coef, core * rows, rows, 0)
    got = lax.ppermute(sent, "core", [(0, 1), (1, 0)])
    first = core == 0
    upper = jnp.concatenate([jnp.where(first, kept, got), jnp.where(first, got, kept)], 1)

    chip = (owners // 2) % SIZES["z"] * SIZES["yhi"] + owners // (2 * SIZES["z"])
    side = jnp.where(owners % 2 == core, 0, width)
    chunk = jnp.concatenate(
        [
            lax.dynamic_slice(pieces, (chip[p], 0, side[p]), (1, rows // chips, width))[0]
            for p in range(PANELS)
        ],
        axis=1,
    )
    copies = jnp.broadcast_to(chunk[None], (chips,) + chunk.shape)
    gathered = lax.all_to_all(copies, CHIPS, 0, 0, tiled=True).reshape(rows, PANELS * width)

    share = lax.dot_general(
        gathered, upper, (((0,), (0,)), ((), ())), preferred_element_type=F32
    ).astype(BF16)
    lowers, uppers = share.shape
    share = jnp.concatenate([share[:, : uppers // 2], share[:, uppers // 2 :]], 0)
    shares = lax.all_to_all(share, ("core",) + BASIS, 0, 0, tiled=True)
    shares = shares.reshape(2 * lax.axis_size(BASIS), -1, uppers // 2)
    moments = jnp.sum(shares.astype(F32), axis=0)
    nu = upper_energy[None, :] - lower_energy[:, None]
    intensity = moments * moments * nu * jnp.exp(-lower_energy)[:, None] * (1.0 - jnp.exp(-nu))
    return moments, intensity


def solution(mesh):
    fine = Mesh(mesh.devices.reshape(tuple(SIZES.values())), tuple(SIZES))
    placed = (
        P(BASIS, STATE),
        P(BASIS, STATE),
        P(),
        P(BASIS, None, None, None),
        P(BASIS, None),
        P(BASIS),
        P(STATE),
    )
    return jax.shard_map(
        on_device,
        mesh=fine,
        in_specs=placed,
        out_specs=(P(BASIS, STATE), P(BASIS, STATE)),
        check_vma=False,
    )
```

```python
import functools

import jax
import jax.numpy as jnp
from jax import lax
from jax.experimental import pallas as pl
from jax.experimental.pallas import tpu as pltpu
from jax.sharding import Mesh
from jax.sharding import PartitionSpec as P

BS = 128
REACH = 2
PANELS = 4
BF16 = jnp.bfloat16
F32 = jnp.float32

SIZES = {"yhi": 4, "z": 8, "core": 2, "ylo": 2, "x": 4}
STATE = ("yhi", "z", "core")
BASIS = ("ylo", "x")
CHIPS = ("z", "yhi")
SWAP = [(0, 1), (1, 0)]

VMEM = pl.BlockSpec(memory_space=pltpu.VMEM)
HBM = pl.BlockSpec(memory_space=pltpu.HBM)
SMEM = pl.BlockSpec(memory_space=pltpu.SMEM)


def half_kernel(
    core_ref, offsets_ref, store, other, own_edge, other_edge, dipole, half, own, terms_in, near,
    own_sem, dipole_sem,
):
    nblk, terms = dipole.shape[0], dipole.shape[1]
    width = own.shape[1]
    first = core_ref[0] * (nblk // 2)
    own_copy = pltpu.make_async_copy(store, own, own_sem)
    own_copy.start()
    copies = [
        pltpu.make_async_copy(dipole.at[first + j], terms_in.at[j], dipole_sem.at[j])
        for j in range(nblk // 2)
    ]
    for copy in copies:
        copy.start()
    own_copy.wait()

    for j in range(nblk // 2):
        column = first + j
        for k in range(terms):
            block = column + offsets_ref[column, k]
            inside = (block >= 0) & (block < nblk)
            rows = pl.ds(k * BS, BS)

            @pl.when(inside)
            def _():
                source = pl.ds(pl.multiple_of(jnp.clip(block, 0, nblk - 1) * BS, BS), BS)
                near[j % 2, rows, :width] = own[source, :]
                near[j % 2, rows, width:] = other[source, :]

            @pl.when(jnp.logical_not(inside))
            def _():
                place = jnp.where(block < 0, block + REACH, block - nblk)
                source = pl.ds(pl.multiple_of(jnp.clip(place, 0, REACH - 1) * BS, BS), BS)
                near[j % 2, rows, :width] = own_edge[source, :]
                near[j % 2, rows, width:] = other_edge[source, :]

        copies[j].wait()
        half[pl.ds(j * BS, BS), :] = lax.dot_general(
            terms_in[j].reshape(terms * BS, BS),
            near[j % 2],
            (((0,), (0,)), ((), ())),
            preferred_element_type=F32,
        ).astype(BF16)


def chip_half(store, dipole, offsets, core):
    rows, width = store.shape
    reach = REACH * BS
    count = lax.axis_size(BASIS)

    def member(basis, kind):
        return basis + count * kind

    own_pairs = [(member(b, 0), member(b + 1, 0)) for b in range(count - 1)]
    own_pairs += [(member(b + 1, 1), member(b, 1)) for b in range(count - 1)]
    other_pairs = [(member(b, 1), member(b + 1, 0)) for b in range(count - 1)]
    other_pairs += [(member(b + 1, 0), member(b, 1)) for b in range(count - 1)]
    axes = ("core",) + BASIS
    low, high = store[:reach], store[rows - reach :]
    first = core == 0
    own_edge = lax.ppermute(jnp.where(first, high, low), axes, own_pairs)
    other_edge = lax.ppermute(jnp.where(first, low, high), axes, other_pairs)
    other = lax.ppermute(store, "core", SWAP)
    nblk, terms = offsets.shape
    return pl.pallas_call(
        half_kernel,
        out_shape=jax.ShapeDtypeStruct((nblk // 2 * BS, 2 * width), BF16),
        in_specs=[SMEM, SMEM, HBM, VMEM, VMEM, VMEM, HBM],
        out_specs=VMEM,
        scratch_shapes=[
            pltpu.VMEM(store.shape, BF16),
            pltpu.VMEM((nblk // 2,) + dipole.shape[1:], BF16),
            pltpu.VMEM((2, terms * BS, 2 * width), BF16),
            pltpu.SemaphoreType.DMA,
            pltpu.SemaphoreType.DMA((nblk // 2,)),
        ],
        compiler_params=pltpu.CompilerParams(vmem_limit_bytes=12 << 20),
        cost_estimate=pl.CostEstimate(
            flops=nblk * terms * BS * BS * 2 * width, bytes_accessed=6 << 20, transcendentals=0
        ),
    )(core.reshape(1), offsets, store, other, own_edge, other_edge, dipole)


def pick_kernel(core_ref, owners_ref, pieces, along, copies, chunk):
    width = pieces.shape[2] // 2
    split = along.shape[0]
    for p in range(PANELS):
        owner = owners_ref[p]
        chip = (owner // 2) % SIZES["z"] * SIZES["yhi"] + owner // (2 * SIZES["z"])
        piece = pieces[chip]
        mine = owner % 2 == core_ref[0]
        chunk[:, pl.ds(p * width, width)] = jnp.where(mine, piece[:, :width], piece[:, width:])
    along[...] = chunk[:split]
    for i in range(copies.shape[0]):
        copies[i] = chunk[split:]


def on_device(upper_coef, store, owners, dipole, offsets, lower_energy, upper_energy):
    core = lax.axis_index("core")
    width = store.shape[1]
    half = chip_half(store, dipole, offsets, core)
    nz, ny = SIZES["z"], SIZES["yhi"]
    rows = half.shape[0]
    piece = rows // (nz * ny)
    split = piece // 2

    pieces = lax.all_to_all(half, CHIPS, 0, 0, tiled=True).reshape(nz * ny, piece, 2 * width)

    lowers = PANELS * width
    along, copies = pl.pallas_call(
        pick_kernel,
        out_shape=(
            jax.ShapeDtypeStruct((split, lowers), BF16),
            jax.ShapeDtypeStruct((nz, piece - split, lowers), BF16),
        ),
        in_specs=[SMEM, SMEM, VMEM],
        out_specs=(VMEM, VMEM),
        scratch_shapes=[pltpu.VMEM((piece, lowers), BF16)],
        compiler_params=pltpu.CompilerParams(vmem_limit_bytes=8 << 20),
        cost_estimate=pl.CostEstimate(flops=0, bytes_accessed=1 << 20, transcendentals=0),
    )(core.reshape(1), owners, pieces)

    b = lax.all_to_all(copies.reshape(-1, lowers), "z", 0, 0, tiled=True)
    a = lax.all_gather(along, "yhi", axis=0, tiled=True)
    a, b = lax.optimization_barrier((a, b))
    b = jnp.broadcast_to(b[None], (ny,) + b.shape).reshape(-1, lowers)
    b = lax.all_to_all(b, "yhi", 0, 0, tiled=True)
    a = lax.all_gather(a, "z", axis=0, tiled=True)

    sent = lax.dynamic_slice_in_dim(upper_coef, (1 - core) * rows, rows, 0)
    kept = lax.dynamic_slice_in_dim(upper_coef, core * rows, rows, 0)
    got = lax.ppermute(sent, "core", SWAP)
    first = core == 0
    upper = jnp.concatenate([jnp.where(first, kept, got), jnp.where(first, got, kept)], 1)
    uppers = upper_coef.shape[1]
    upper = upper.reshape(nz, ny, piece, 2 * uppers)
    upper_a = upper[:, :, :split].reshape(-1, 2 * uppers)
    upper_b = jnp.swapaxes(upper[:, :, split:], 0, 1).reshape(-1, 2 * uppers)
    dot = functools.partial(
        lax.dot_general,
        dimension_numbers=(((0,), (0,)), ((), ())),
        preferred_element_type=F32,
    )
    share = (dot(a, upper_a) + dot(b, upper_b)).astype(BF16)
    share = jnp.concatenate([share[:, :uppers], share[:, uppers:]], 0)
    shares = lax.all_to_all(share, ("core",) + BASIS, 0, 0, tiled=True)
    shares = shares.reshape(2 * lax.axis_size(BASIS), -1, uppers)
    moments = jnp.sum(shares.astype(F32), axis=0)
    nu = upper_energy[None, :] - lower_energy[:, None]
    intensity = moments * moments * nu * jnp.exp(-lower_energy)[:, None] * (1.0 - jnp.exp(-nu))
    return moments, intensity


def solution(mesh):
    fine = Mesh(mesh.devices.reshape(tuple(SIZES.values())), tuple(SIZES))
    placed = (
        P(BASIS, STATE),
        P(BASIS, STATE),
        P(),
        P(BASIS, None, None, None),
        P(BASIS, None),
        P(BASIS),
        P(STATE),
    )
    return jax.shard_map(
        on_device,
        mesh=fine,
        in_specs=placed,
        out_specs=(P(BASIS, STATE), P(BASIS, STATE)),
        check_vma=False,
    )
```

```python
import jax
import jax.numpy as jnp
from jax import lax
from jax.experimental import pallas as pl
from jax.experimental.pallas import tpu as pltpu
from jax.sharding import Mesh
from jax.sharding import PartitionSpec as P

BS = 128
REACH = 2
PANELS = 4
BF16 = jnp.bfloat16
F32 = jnp.float32

SIZES = {"yhi": 4, "zhi": 4, "zlo": 2, "core": 2, "ylo": 2, "x": 4}
STATE = ("yhi", "zhi", "zlo", "core")
BASIS = ("ylo", "x")
SHARED = ("core", "zlo")
GATHER = ("zhi", "yhi")
CHIPS = ("zlo",) + GATHER
SWAP = [(0, 1), (1, 0)]

VMEM = pl.BlockSpec(memory_space=pltpu.VMEM)
HBM = pl.BlockSpec(memory_space=pltpu.HBM)
SMEM = pl.BlockSpec(memory_space=pltpu.SMEM)


def half_kernel(
    core_ref, offsets_ref, store, other, own_edge, other_edge, dipole, half, near, terms_in,
    near_sem, dipole_sem,
):
    nblk, terms = dipole.shape[0], dipole.shape[1]
    rows, width = store.shape
    reach = REACH * BS
    core = core_ref[0]
    first = core * (nblk // 2)
    edge = pl.ds(pl.multiple_of(core * (reach + rows), BS), reach)
    middle = pl.ds(reach, rows)
    left, right = pl.ds(0, width), pl.ds(width, width)
    fills = [
        pltpu.make_async_copy(source, near.at[place, lanes], near_sem.at[i])
        for i, (source, place, lanes) in enumerate(
            [
                (store, middle, left),
                (other, middle, right),
                (own_edge, edge, left),
                (other_edge, edge, right),
            ]
        )
    ]
    copies = [
        pltpu.make_async_copy(dipole.at[first + j], terms_in.at[j], dipole_sem.at[j])
        for j in range(nblk // 2)
    ]
    for copy in fills + copies:
        copy.start()
    for copy in fills:
        copy.wait()

    for j in range(nblk // 2):
        column = first + j
        blocks = []
        for k in range(terms):
            block = column + offsets_ref[column, k] + REACH
            blocks.append(near[pl.ds(pl.multiple_of(block * BS, BS), BS), :])
        copies[j].wait()
        half[pl.ds(j * BS, BS), :] = lax.dot_general(
            terms_in[j].reshape(terms * BS, BS),
            jnp.concatenate(blocks, axis=0),
            (((0,), (0,)), ((), ())),
            preferred_element_type=F32,
        ).astype(BF16)


def chip_half(store, dipole, offsets, core):
    rows, width = store.shape
    reach = REACH * BS
    count = lax.axis_size(BASIS)

    def member(basis, kind):
        return basis + count * kind

    own_pairs = [(member(b, 0), member(b + 1, 0)) for b in range(count - 1)]
    own_pairs += [(member(b + 1, 1), member(b, 1)) for b in range(count - 1)]
    other_pairs = [(member(b, 1), member(b + 1, 0)) for b in range(count - 1)]
    other_pairs += [(member(b + 1, 0), member(b, 1)) for b in range(count - 1)]
    axes = ("core",) + BASIS
    low, high = store[:reach], store[rows - reach :]
    first = core == 0
    own_edge = lax.ppermute(jnp.where(first, high, low), axes, own_pairs)
    other_edge = lax.ppermute(jnp.where(first, low, high), axes, other_pairs)
    other = lax.ppermute(store, "core", SWAP)
    nblk, terms = offsets.shape
    return pl.pallas_call(
        half_kernel,
        out_shape=jax.ShapeDtypeStruct((nblk // 2 * BS, 2 * width), BF16),
        in_specs=[SMEM, SMEM, HBM, HBM, HBM, HBM, HBM],
        out_specs=VMEM,
        scratch_shapes=[
            pltpu.VMEM((rows + 2 * reach, 2 * width), BF16),
            pltpu.VMEM((nblk // 2,) + dipole.shape[1:], BF16),
            pltpu.SemaphoreType.DMA((4,)),
            pltpu.SemaphoreType.DMA((nblk // 2,)),
        ],
        compiler_params=pltpu.CompilerParams(vmem_limit_bytes=12 << 20),
        cost_estimate=pl.CostEstimate(
            flops=nblk * terms * BS * BS * 2 * width, bytes_accessed=6 << 20, transcendentals=0
        ),
    )(core.reshape(1), offsets, store, other, own_edge, other_edge, dipole)


def pick_kernel(core_ref, owners_ref, pieces, copies, chunk):
    width = pieces.shape[2] // 2
    for p in range(PANELS):
        owner = owners_ref[p]
        zlo, zhi, yhi = owner // 2 % 2, owner // 4 % SIZES["zhi"], owner // 16
        piece = pieces[(zlo * SIZES["zhi"] + zhi) * SIZES["yhi"] + yhi]
        mine = owner % 2 == core_ref[0]
        chunk[:, pl.ds(p * width, width)] = jnp.where(mine, piece[:, :width], piece[:, width:])
    for i in range(copies.shape[0]):
        copies[i] = chunk[...]


def on_device(upper_coef, store, owners, dipole, offsets, lower_energy, upper_energy):
    core = lax.axis_index("core")
    width = store.shape[1]
    uppers = upper_coef.shape[1]
    upper = lax.all_to_all(upper_coef, SHARED, 0, 0, tiled=True)
    upper = upper.reshape(2, 2, -1, uppers)

    half = chip_half(store, dipole, offsets, core)
    half, upper = lax.optimization_barrier((half, upper))
    chips, peers = lax.axis_size(CHIPS), lax.axis_size(GATHER)
    rows = half.shape[0] // chips
    lowers = PANELS * width
    pieces = lax.all_to_all(half, CHIPS, 0, 0, tiled=True).reshape(chips, rows, 2 * width)

    copies = pl.pallas_call(
        pick_kernel,
        out_shape=jax.ShapeDtypeStruct((peers, rows, lowers), BF16),
        in_specs=[SMEM, SMEM, VMEM],
        out_specs=VMEM,
        scratch_shapes=[pltpu.VMEM((rows, lowers), BF16)],
        compiler_params=pltpu.CompilerParams(vmem_limit_bytes=8 << 20),
        cost_estimate=pl.CostEstimate(flops=0, bytes_accessed=1 << 20, transcendentals=0),
    )(core.reshape(1), owners, pieces)
    gathered = lax.all_to_all(copies.reshape(-1, lowers), GATHER, 0, 0, tiled=True)

    def share(kind, member):
        rhs = lax.dynamic_index_in_dim(upper, kind, 0, keepdims=False)[member]
        return lax.dot_general(
            gathered, rhs, (((0,), (0,)), ((), ())), preferred_element_type=F32
        )

    received = [
        lax.ppermute(share(1 - core, m).astype(BF16), "core", SWAP) for m in range(2)
    ]
    added = [(share(core, m) + received[m].astype(F32)).astype(BF16) for m in range(2)]
    shares = lax.all_to_all(jnp.concatenate(added, 0), ("zlo",) + BASIS, 0, 0, tiled=True)
    shares = shares.reshape(2 * lax.axis_size(BASIS), -1, uppers)
    moments = jnp.sum(shares.astype(F32), axis=0)
    nu = upper_energy[None, :] - lower_energy[:, None]
    intensity = moments * moments * nu * jnp.exp(-lower_energy)[:, None] * (1.0 - jnp.exp(-nu))
    return moments, intensity


def solution(mesh):
    fine = Mesh(mesh.devices.reshape(tuple(SIZES.values())), tuple(SIZES))
    placed = (
        P(BASIS, STATE),
        P(BASIS, STATE),
        P(),
        P(BASIS, None, None, None),
        P(BASIS, None),
        P(BASIS),
        P(STATE),
    )
    return jax.shard_map(
        on_device,
        mesh=fine,
        in_specs=placed,
        out_specs=(P(BASIS, STATE), P(BASIS, STATE)),
        check_vma=False,
    )
```

```python
import jax
import jax.numpy as jnp
from jax import lax
from jax.experimental import pallas as pl
from jax.experimental.pallas import tpu as pltpu
from jax.sharding import Mesh
from jax.sharding import PartitionSpec as P

BS = 128
REACH = 2
PANELS = 4
BF16 = jnp.bfloat16
F32 = jnp.float32

SIZES = {"yhi": 4, "zhi": 4, "zlo": 2, "core": 2, "ylo": 2, "x": 4}
STATE = ("yhi", "zhi", "zlo", "core")
BASIS = ("ylo", "x")
SHARED = ("core", "zlo")
GATHER = ("yhi", "zhi")
CHIPS = ("zlo",) + GATHER
SWAP = [(0, 1), (1, 0)]

VMEM = pl.BlockSpec(memory_space=pltpu.VMEM)
HBM = pl.BlockSpec(memory_space=pltpu.HBM)
SMEM = pl.BlockSpec(memory_space=pltpu.SMEM)


def half_kernel(
    core_ref, offsets_ref, store, other, own_edge, other_edge, dipole, half, near, terms_in,
    near_sem, dipole_sem,
):
    nblk, terms = dipole.shape[0], dipole.shape[1]
    rows, width = store.shape
    reach = REACH * BS
    core = core_ref[0]
    first = core * (nblk // 2)
    edge = pl.ds(pl.multiple_of(core * (reach + rows), BS), reach)
    middle = pl.ds(reach, rows)
    left, right = pl.ds(0, width), pl.ds(width, width)
    fills = [
        pltpu.make_async_copy(source, near.at[place, lanes], near_sem.at[i])
        for i, (source, place, lanes) in enumerate(
            [
                (store, middle, left),
                (other, middle, right),
                (own_edge, edge, left),
                (other_edge, edge, right),
            ]
        )
    ]
    copies = [
        pltpu.make_async_copy(dipole.at[first + j], terms_in.at[j], dipole_sem.at[j])
        for j in range(nblk // 2)
    ]
    for copy in fills + copies:
        copy.start()
    for copy in fills:
        copy.wait()

    for j in range(nblk // 2):
        column = first + j
        blocks = []
        for k in range(terms):
            block = column + offsets_ref[column, k] + REACH
            blocks.append(near[pl.ds(pl.multiple_of(block * BS, BS), BS), :])
        copies[j].wait()
        half[pl.ds(j * BS, BS), :] = lax.dot_general(
            terms_in[j].reshape(terms * BS, BS),
            jnp.concatenate(blocks, axis=0),
            (((0,), (0,)), ((), ())),
            preferred_element_type=F32,
        ).astype(BF16)


def chip_half(store, dipole, offsets, core):
    rows, width = store.shape
    reach = REACH * BS
    count = lax.axis_size(BASIS)

    def member(basis, kind):
        return basis + count * kind

    own_pairs = [(member(b, 0), member(b + 1, 0)) for b in range(count - 1)]
    own_pairs += [(member(b + 1, 1), member(b, 1)) for b in range(count - 1)]
    other_pairs = [(member(b, 1), member(b + 1, 0)) for b in range(count - 1)]
    other_pairs += [(member(b + 1, 0), member(b, 1)) for b in range(count - 1)]
    axes = ("core",) + BASIS
    low, high = store[:reach], store[rows - reach :]
    first = core == 0
    own_edge = lax.ppermute(jnp.where(first, high, low), axes, own_pairs)
    other_edge = lax.ppermute(jnp.where(first, low, high), axes, other_pairs)
    other = lax.ppermute(store, "core", SWAP)
    nblk, terms = offsets.shape
    return pl.pallas_call(
        half_kernel,
        out_shape=jax.ShapeDtypeStruct((nblk // 2 * BS, 2 * width), BF16),
        in_specs=[SMEM, SMEM, HBM, HBM, HBM, HBM, HBM],
        out_specs=VMEM,
        scratch_shapes=[
            pltpu.VMEM((rows + 2 * reach, 2 * width), BF16),
            pltpu.VMEM((nblk // 2,) + dipole.shape[1:], BF16),
            pltpu.SemaphoreType.DMA((4,)),
            pltpu.SemaphoreType.DMA((nblk // 2,)),
        ],
        compiler_params=pltpu.CompilerParams(vmem_limit_bytes=12 << 20),
        cost_estimate=pl.CostEstimate(
            flops=nblk * terms * BS * BS * 2 * width, bytes_accessed=6 << 20, transcendentals=0
        ),
    )(core.reshape(1), offsets, store, other, own_edge, other_edge, dipole)


def pick_kernel(core_ref, owners_ref, pieces, copies, chunk):
    width = pieces.shape[2] // 2
    for p in range(PANELS):
        owner = owners_ref[p]
        zlo, zhi, yhi = owner // 2 % 2, owner // 4 % SIZES["zhi"], owner // 16
        piece = pieces[(zlo * SIZES["yhi"] + yhi) * SIZES["zhi"] + zhi]
        mine = owner % 2 == core_ref[0]
        chunk[:, pl.ds(p * width, width)] = jnp.where(mine, piece[:, :width], piece[:, width:])
    for i in range(copies.shape[0]):
        copies[i] = chunk[...]


def on_device(upper_coef, store, owners, dipole, offsets, lower_energy, upper_energy):
    core = lax.axis_index("core")
    width = store.shape[1]
    uppers = upper_coef.shape[1]
    upper = lax.all_to_all(upper_coef, SHARED, 0, 0, tiled=True)
    upper = upper.reshape(2, 2, -1, uppers)

    half = chip_half(store, dipole, offsets, core)
    half, upper = lax.optimization_barrier((half, upper))
    chips, peers = lax.axis_size(CHIPS), lax.axis_size(GATHER)
    rows = half.shape[0] // chips
    lowers = PANELS * width
    pieces = lax.all_to_all(half, CHIPS, 0, 0, tiled=True).reshape(chips, rows, 2 * width)

    copies = pl.pallas_call(
        pick_kernel,
        out_shape=jax.ShapeDtypeStruct((peers, rows, lowers), BF16),
        in_specs=[SMEM, SMEM, VMEM],
        out_specs=VMEM,
        scratch_shapes=[pltpu.VMEM((rows, lowers), BF16)],
        compiler_params=pltpu.CompilerParams(vmem_limit_bytes=8 << 20),
        cost_estimate=pl.CostEstimate(flops=0, bytes_accessed=1 << 20, transcendentals=0),
    )(core.reshape(1), owners, pieces)
    gathered = lax.all_to_all(copies.reshape(-1, lowers), GATHER, 0, 0, tiled=True)

    def beside(kind):
        blocks = lax.dynamic_index_in_dim(upper, kind, 0, keepdims=False)
        return jnp.concatenate([blocks[0], blocks[1]], 1)

    def share(rhs):
        return lax.dot_general(
            gathered, rhs, (((0,), (0,)), ((), ())), preferred_element_type=F32
        )

    received = lax.ppermute(share(beside(1 - core)).astype(BF16), "core", SWAP)
    kept, received = lax.optimization_barrier((share(beside(core)), received))
    added = (kept + received.astype(F32)).astype(BF16)
    ranges = lax.axis_size(BASIS)
    sides = [added[:, :uppers], added[:, uppers:]]
    added = jnp.stack([side.reshape(ranges, -1, uppers) for side in sides], 1)
    added = added.reshape(2 * lowers, uppers)
    shares = lax.all_to_all(added, BASIS + ("zlo",), 0, 0, tiled=True)
    shares = shares.reshape(2 * ranges, -1, uppers)
    moments = jnp.sum(shares.astype(F32), axis=0)
    nu = upper_energy[None, :] - lower_energy[:, None]
    intensity = moments * moments * nu * jnp.exp(-lower_energy)[:, None] * (1.0 - jnp.exp(-nu))
    return moments, intensity


def solution(mesh):
    fine = Mesh(mesh.devices.reshape(tuple(SIZES.values())), tuple(SIZES))
    placed = (
        P(BASIS, STATE),
        P(BASIS, STATE),
        P(),
        P(BASIS, None, None, None),
        P(BASIS, None),
        P(BASIS),
        P(STATE),
    )
    return jax.shard_map(
        on_device,
        mesh=fine,
        in_specs=placed,
        out_specs=(P(BASIS, STATE), P(BASIS, STATE)),
        check_vma=False,
    )
```

```python
import functools

import jax
import jax.numpy as jnp
from jax import lax
from jax.experimental import pallas as pl
from jax.experimental.pallas import tpu as pltpu
from jax.sharding import Mesh
from jax.sharding import PartitionSpec as P

BS = 128
REACH = 2
PANELS = 4
BF16 = jnp.bfloat16
F32 = jnp.float32

SIZES = {"yhi": 4, "zhi": 4, "zlo": 2, "core": 2, "ylo": 2, "x": 4}
STATE = ("yhi", "zhi", "zlo", "core")
BASIS = ("ylo", "x")
SHARED = ("core", "zlo")
GATHER = ("yhi", "zhi")
CHIPS = ("zlo",) + GATHER
SWAP = [(0, 1), (1, 0)]

VMEM = pl.BlockSpec(memory_space=pltpu.VMEM)
SMEM = pl.BlockSpec(memory_space=pltpu.SMEM)


def owned(owners_ref, state):
    found = owners_ref[0] == state
    for p in range(1, PANELS):
        found = found | (owners_ref[p] == state)
    return found


def half_kernel(
    second, state_ref, owners_ref, offsets_ref, own, other, own_edge, other_edge, dipole, half
):
    nblk, terms = dipole.shape[0], dipole.shape[1]
    ncol = nblk // 2
    core = lax.rem(state_ref[0], 2)
    first = core * ncol
    if second:
        mine = core == 1
    else:
        mine = (core == 0) == owned(owners_ref, state_ref[0] - core)

    for j in range(ncol):
        column = first + j
        blocks = []
        for k in range(terms):
            block = column + offsets_ref[column, k]
            inside = (block >= 0) & (block < nblk)
            block_in = jnp.clip(block, 0, nblk - 1)
            source = pl.ds(pl.multiple_of(block_in * BS, BS), BS)
            rows = jnp.where(mine, own[source, :], other[source, :])
            if j < REACH or j >= ncol - REACH:
                place = jnp.where(block < 0, block + REACH, block - nblk)
                beyond = pl.ds(pl.multiple_of(jnp.clip(place, 0, REACH - 1) * BS, BS), BS)
                edge = jnp.where(mine, own_edge[beyond, :], other_edge[beyond, :])
                rows = jnp.where(inside, rows, edge)
            blocks.append(rows)
        half[pl.ds(j * BS, BS), :] = lax.dot_general(
            dipole[column].reshape(terms * BS, BS),
            jnp.concatenate(blocks, axis=0),
            (((0,), (0,)), ((), ())),
            preferred_element_type=F32,
        ).astype(BF16)


def chip_panels(store, core):
    rows = store.shape[0]
    reach = REACH * BS
    count = lax.axis_size(BASIS)

    def member(basis, kind):
        return basis + count * kind

    own_pairs = [(member(b, 0), member(b + 1, 0)) for b in range(count - 1)]
    own_pairs += [(member(b + 1, 1), member(b, 1)) for b in range(count - 1)]
    other_pairs = [(member(b, 1), member(b + 1, 0)) for b in range(count - 1)]
    other_pairs += [(member(b + 1, 0), member(b, 1)) for b in range(count - 1)]
    axes = ("core",) + BASIS
    low, high = store[:reach], store[rows - reach :]
    first = core == 0
    own_edge = lax.ppermute(jnp.where(first, high, low), axes, own_pairs)
    other_edge = lax.ppermute(jnp.where(first, low, high), axes, other_pairs)
    other = lax.ppermute(store, "core", SWAP)
    return store, other, own_edge, other_edge


def chip_half(second, state, owners, offsets, panels, dipole):
    nblk, terms = offsets.shape
    rows, width = panels[0].shape
    return pl.pallas_call(
        functools.partial(half_kernel, second),
        out_shape=jax.ShapeDtypeStruct((rows // 2, width), BF16),
        in_specs=[SMEM, SMEM, SMEM] + [VMEM] * 5,
        out_specs=VMEM,
        compiler_params=pltpu.CompilerParams(vmem_limit_bytes=12 << 20),
        cost_estimate=pl.CostEstimate(
            flops=nblk * terms * BS * BS * width, bytes_accessed=6 << 20, transcendentals=0
        ),
    )(state.reshape(1), owners, offsets, *panels, dipole)


def pick_kernel(owners_ref, pieces, seconds, copies, chunk):
    width = pieces.shape[2]
    for p in range(PANELS):
        owner = owners_ref[p]
        core, zlo, zhi, yhi = owner % 2, owner // 2 % 2, owner // 4 % SIZES["zhi"], owner // 16
        chip = (zlo * SIZES["yhi"] + yhi) * SIZES["zhi"] + zhi
        late = (core == 1) & owned(owners_ref, owner - 1)
        chunk[:, pl.ds(p * width, width)] = jnp.where(late, seconds[chip], pieces[chip])
    for i in range(copies.shape[0]):
        copies[i] = chunk[...]


def pick(owners, pieces, seconds):
    peers = lax.axis_size(GATHER)
    rows, width = pieces.shape[1:]
    return pl.pallas_call(
        pick_kernel,
        out_shape=jax.ShapeDtypeStruct((peers, rows, PANELS * width), BF16),
        in_specs=[SMEM, VMEM, VMEM],
        out_specs=VMEM,
        scratch_shapes=[pltpu.VMEM((rows, PANELS * width), BF16)],
        compiler_params=pltpu.CompilerParams(vmem_limit_bytes=8 << 20),
        cost_estimate=pl.CostEstimate(flops=0, bytes_accessed=1 << 20, transcendentals=0),
    )(owners, pieces, seconds)


def on_device(upper_coef, store, owners, dipole, offsets, lower_energy, upper_energy):
    core = lax.axis_index("core")
    state = lax.axis_index(STATE)
    width = store.shape[1]
    lowers = PANELS * width
    uppers = upper_coef.shape[1]
    upper = lax.all_to_all(upper_coef, SHARED, 0, 0, tiled=True)
    upper = upper.reshape(2, 2, -1, uppers)

    panels = chip_panels(store, core)
    half = chip_half(False, state, owners, offsets, panels, dipole)
    half, upper = lax.optimization_barrier((half, upper))

    def scatter(half):
        chips = lax.axis_size(CHIPS)
        return lax.all_to_all(half, CHIPS, 0, 0, tiled=True).reshape(chips, -1, width)

    pieces = scatter(half)
    chips_of = owners // 2
    shared = jnp.sum((chips_of[:, None] == chips_of[None, :]).astype(jnp.int32)) > PANELS
    copies = lax.cond(
        shared,
        lambda: pick(
            owners, pieces, scatter(chip_half(True, state, owners, offsets, panels, dipole))
        ),
        lambda: pick(owners, pieces, pieces),
    )
    gathered = lax.all_to_all(copies.reshape(-1, lowers), GATHER, 0, 0, tiled=True)

    def beside(kind):
        blocks = lax.dynamic_index_in_dim(upper, kind, 0, keepdims=False)
        return jnp.concatenate([blocks[0], blocks[1]], 1)

    def share(rhs):
        return lax.dot_general(
            gathered, rhs, (((0,), (0,)), ((), ())), preferred_element_type=F32
        )

    received = lax.ppermute(share(beside(1 - core)).astype(BF16), "core", SWAP)
    kept, received = lax.optimization_barrier((share(beside(core)), received))
    added = (kept + received.astype(F32)).astype(BF16)
    ranges = lax.axis_size(BASIS)
    sides = [added[:, :uppers], added[:, uppers:]]
    added = jnp.stack([side.reshape(ranges, -1, uppers) for side in sides], 1)
    added = added.reshape(2 * lowers, uppers)
    shares = lax.all_to_all(added, BASIS + ("zlo",), 0, 0, tiled=True)
    shares = shares.reshape(2 * ranges, -1, uppers)
    moments = jnp.sum(shares.astype(F32), axis=0)
    nu = upper_energy[None, :] - lower_energy[:, None]
    intensity = moments * moments * nu * jnp.exp(-lower_energy)[:, None] * (1.0 - jnp.exp(-nu))
    return moments, intensity


def solution(mesh):
    fine = Mesh(mesh.devices.reshape(tuple(SIZES.values())), tuple(SIZES))
    placed = (
        P(BASIS, STATE),
        P(BASIS, STATE),
        P(),
        P(BASIS, None, None, None),
        P(BASIS, None),
        P(BASIS),
        P(STATE),
    )
    return jax.shard_map(
        on_device,
        mesh=fine,
        in_specs=placed,
        out_specs=(P(BASIS, STATE), P(BASIS, STATE)),
        check_vma=False,
    )
```

```python
import functools

import jax
import jax.numpy as jnp
from jax import lax
from jax.experimental import pallas as pl
from jax.experimental.pallas import tpu as pltpu
from jax.sharding import Mesh
from jax.sharding import PartitionSpec as P

BS = 128
REACH = 2
PANELS = 4
BF16 = jnp.bfloat16
F32 = jnp.float32

SIZES = {"yhi": 4, "zhi": 4, "zlo": 2, "core": 2, "ylo": 2, "x": 4}
STATE = ("yhi", "zhi", "zlo", "core")
BASIS = ("ylo", "x")
SHARED = ("zlo", "core")
GATHER = ("yhi", "zhi")
CHIPS = ("zlo",) + GATHER
SWAP = [(0, 1), (1, 0)]

VMEM = pl.BlockSpec(memory_space=pltpu.VMEM)
SMEM = pl.BlockSpec(memory_space=pltpu.SMEM)


def owned(owners_ref, state):
    found = owners_ref[0] == state
    for p in range(1, PANELS):
        found = found | (owners_ref[p] == state)
    return found


def half_kernel(
    second, state_ref, owners_ref, offsets_ref, own, other, own_edge, other_edge, dipole, half
):
    nblk, terms = dipole.shape[0], dipole.shape[1]
    ncol = nblk // 2
    core = lax.rem(state_ref[0], 2)
    first = core * ncol
    if second:
        mine = core == 1
    else:
        mine = (core == 0) == owned(owners_ref, state_ref[0] - core)

    for j in range(ncol):
        column = first + j
        blocks = []
        for k in range(terms):
            block = column + offsets_ref[column, k]
            inside = (block >= 0) & (block < nblk)
            block_in = jnp.clip(block, 0, nblk - 1)
            source = pl.ds(pl.multiple_of(block_in * BS, BS), BS)
            rows = jnp.where(mine, own[source, :], other[source, :])
            if j < REACH or j >= ncol - REACH:
                place = jnp.where(block < 0, block + REACH, block - nblk)
                beyond = pl.ds(pl.multiple_of(jnp.clip(place, 0, REACH - 1) * BS, BS), BS)
                edge = jnp.where(mine, own_edge[beyond, :], other_edge[beyond, :])
                rows = jnp.where(inside, rows, edge)
            blocks.append(rows)
        half[pl.ds(j * BS, BS), :] = lax.dot_general(
            dipole[column].reshape(terms * BS, BS),
            jnp.concatenate(blocks, axis=0),
            (((0,), (0,)), ((), ())),
            preferred_element_type=F32,
        ).astype(BF16)


def chip_panels(store, core):
    rows = store.shape[0]
    reach = REACH * BS
    count = lax.axis_size(BASIS)

    def member(basis, kind):
        return basis + count * kind

    own_pairs = [(member(b, 0), member(b + 1, 0)) for b in range(count - 1)]
    own_pairs += [(member(b + 1, 1), member(b, 1)) for b in range(count - 1)]
    other_pairs = [(member(b, 1), member(b + 1, 0)) for b in range(count - 1)]
    other_pairs += [(member(b + 1, 0), member(b, 1)) for b in range(count - 1)]
    axes = ("core",) + BASIS
    low, high = store[:reach], store[rows - reach :]
    first = core == 0
    own_edge = lax.ppermute(jnp.where(first, high, low), axes, own_pairs)
    other_edge = lax.ppermute(jnp.where(first, low, high), axes, other_pairs)
    other = lax.ppermute(store, "core", SWAP)
    return store, other, own_edge, other_edge


def chip_half(second, state, owners, offsets, panels, dipole):
    nblk, terms = offsets.shape
    rows, width = panels[0].shape
    return pl.pallas_call(
        functools.partial(half_kernel, second),
        out_shape=jax.ShapeDtypeStruct((rows // 2, width), BF16),
        in_specs=[SMEM, SMEM, SMEM] + [VMEM] * 5,
        out_specs=VMEM,
        compiler_params=pltpu.CompilerParams(vmem_limit_bytes=12 << 20),
        cost_estimate=pl.CostEstimate(
            flops=nblk * terms * BS * BS * width, bytes_accessed=6 << 20, transcendentals=0
        ),
    )(state.reshape(1), owners, offsets, *panels, dipole)


def pick_kernel(owners_ref, pieces, seconds, copies, chunk):
    width = pieces.shape[2]
    for p in range(PANELS):
        owner = owners_ref[p]
        core, zlo, zhi, yhi = owner % 2, owner // 2 % 2, owner // 4 % SIZES["zhi"], owner // 16
        chip = (zlo * SIZES["yhi"] + yhi) * SIZES["zhi"] + zhi
        late = (core == 1) & owned(owners_ref, owner - 1)
        chunk[:, pl.ds(p * width, width)] = jnp.where(late, seconds[chip], pieces[chip])
    for i in range(copies.shape[0]):
        copies[i] = chunk[...]


def pick(owners, pieces, seconds):
    peers = lax.axis_size(GATHER)
    rows, width = pieces.shape[1:]
    return pl.pallas_call(
        pick_kernel,
        out_shape=jax.ShapeDtypeStruct((peers, rows, PANELS * width), BF16),
        in_specs=[SMEM, VMEM, VMEM],
        out_specs=VMEM,
        scratch_shapes=[pltpu.VMEM((rows, PANELS * width), BF16)],
        compiler_params=pltpu.CompilerParams(vmem_limit_bytes=8 << 20),
        cost_estimate=pl.CostEstimate(flops=0, bytes_accessed=1 << 20, transcendentals=0),
    )(owners, pieces, seconds)


def on_device(upper_coef, store, owners, dipole, offsets, lower_energy, upper_energy):
    core = lax.axis_index("core")
    state = lax.axis_index(STATE)
    width = store.shape[1]
    lowers = PANELS * width
    uppers = upper_coef.shape[1]
    zlo = lax.axis_index("zlo")
    quarter = upper_coef.shape[0] // 4

    def mine(flip_zlo, flip_core):
        start = ((core ^ flip_core) * 2 + (zlo ^ flip_zlo)) * quarter
        return lax.dynamic_slice_in_dim(upper_coef, start, quarter, 0)

    def from_peer(flip_zlo, flip_core):
        flip = 2 * flip_zlo + flip_core
        return lax.ppermute(mine(flip_zlo, flip_core), SHARED, [(i, i ^ flip) for i in range(4)])

    def beside(near, far):
        low = zlo == 0
        return jnp.concatenate([jnp.where(low, near, far), jnp.where(low, far, near)], 1)

    kinds = [from_peer(1, 1), from_peer(1, 0), from_peer(0, 1)]
    panels = chip_panels(store, core)
    half = chip_half(False, state, owners, offsets, panels, dipole)

    half, kinds[1] = lax.optimization_barrier((half, kinds[1]))

    def scatter(half):
        chips = lax.axis_size(CHIPS)
        return lax.all_to_all(half, CHIPS, 0, 0, tiled=True).reshape(chips, -1, width)

    pieces = scatter(half)
    pieces, kinds[0], kinds[2] = lax.optimization_barrier((pieces, kinds[0], kinds[2]))
    chips_of = owners // 2
    shared = jnp.sum((chips_of[:, None] == chips_of[None, :]).astype(jnp.int32)) > PANELS
    copies = lax.cond(
        shared,
        lambda: pick(
            owners, pieces, scatter(chip_half(True, state, owners, offsets, panels, dipole))
        ),
        lambda: pick(owners, pieces, pieces),
    )
    gathered = lax.all_to_all(copies.reshape(-1, lowers), GATHER, 0, 0, tiled=True)

    upper_other = beside(kinds[2], kinds[0])
    upper_own = beside(mine(0, 0), kinds[1])

    def share(rhs):
        return lax.dot_general(
            gathered, rhs, (((0,), (0,)), ((), ())), preferred_element_type=F32
        )

    received = lax.ppermute(share(upper_other).astype(BF16), "core", SWAP)
    kept, received = lax.optimization_barrier((share(upper_own), received))
    added = (kept + received.astype(F32)).astype(BF16)
    ranges = lax.axis_size(BASIS)
    sides = [added[:, :uppers], added[:, uppers:]]
    added = jnp.stack([side.reshape(ranges, -1, uppers) for side in sides], 1)
    added = added.reshape(2 * lowers, uppers)
    shares = lax.all_to_all(added, BASIS + ("zlo",), 0, 0, tiled=True)
    shares = shares.reshape(2 * ranges, -1, uppers)
    moments = jnp.sum(shares.astype(F32), axis=0)
    nu = upper_energy[None, :] - lower_energy[:, None]
    intensity = moments * moments * nu * jnp.exp(-lower_energy)[:, None] * (1.0 - jnp.exp(-nu))
    return moments, intensity


def solution(mesh):
    fine = Mesh(mesh.devices.reshape(tuple(SIZES.values())), tuple(SIZES))
    placed = (
        P(BASIS, STATE),
        P(BASIS, STATE),
        P(),
        P(BASIS, None, None, None),
        P(BASIS, None),
        P(BASIS),
        P(STATE),
    )
    return jax.shard_map(
        on_device,
        mesh=fine,
        in_specs=placed,
        out_specs=(P(BASIS, STATE), P(BASIS, STATE)),
        check_vma=False,
    )
```

```python
import functools

import jax
import jax.numpy as jnp
from jax import lax
from jax.experimental import pallas as pl
from jax.experimental.pallas import tpu as pltpu
from jax.sharding import Mesh
from jax.sharding import PartitionSpec as P

BS = 128
REACH = 2
PANELS = 4
BF16 = jnp.bfloat16
F32 = jnp.float32

SIZES = {"yhi": 4, "zhi": 4, "zlo": 2, "core": 2, "ylo": 2, "x": 4}
STATE = ("yhi", "zhi", "zlo", "core")
BASIS = ("ylo", "x")
SHARED = ("zlo", "core")
GATHER = ("yhi", "zhi")
CHIPS = ("zlo",) + GATHER
SWAP = [(0, 1), (1, 0)]

VMEM = pl.BlockSpec(memory_space=pltpu.VMEM)
SMEM = pl.BlockSpec(memory_space=pltpu.SMEM)


def owned(owners_ref, state):
    found = owners_ref[0] == state
    for p in range(1, PANELS):
        found = found | (owners_ref[p] == state)
    return found


def half_kernel(
    second, state_ref, owners_ref, offsets_ref, own, other, own_edge, other_edge, dipole, half
):
    nblk, terms = dipole.shape[0], dipole.shape[1]
    ncol = nblk // 2
    core = lax.rem(state_ref[0], 2)
    first = core * ncol
    if second:
        mine = core == 1
    else:
        mine = (core == 0) == owned(owners_ref, state_ref[0] - core)

    for j in range(ncol):
        column = first + j
        blocks = []
        for k in range(terms):
            block = column + offsets_ref[column, k]
            inside = (block >= 0) & (block < nblk)
            block_in = jnp.clip(block, 0, nblk - 1)
            source = pl.ds(pl.multiple_of(block_in * BS, BS), BS)
            rows = jnp.where(mine, own[source, :], other[source, :])
            if j < REACH or j >= ncol - REACH:
                place = jnp.where(block < 0, block + REACH, block - nblk)
                beyond = pl.ds(pl.multiple_of(jnp.clip(place, 0, REACH - 1) * BS, BS), BS)
                edge = jnp.where(mine, own_edge[beyond, :], other_edge[beyond, :])
                rows = jnp.where(inside, rows, edge)
            blocks.append(rows)
        half[pl.ds(j * BS, BS), :] = lax.dot_general(
            dipole[column].reshape(terms * BS, BS),
            jnp.concatenate(blocks, axis=0),
            (((0,), (0,)), ((), ())),
            preferred_element_type=F32,
        ).astype(BF16)


def chip_panels(store, core):
    rows = store.shape[0]
    reach = REACH * BS
    count = lax.axis_size(BASIS)

    def member(basis, kind):
        return basis + count * kind

    own_pairs = [(member(b, 0), member(b + 1, 0)) for b in range(count - 1)]
    own_pairs += [(member(b + 1, 1), member(b, 1)) for b in range(count - 1)]
    other_pairs = [(member(b, 1), member(b + 1, 0)) for b in range(count - 1)]
    other_pairs += [(member(b + 1, 0), member(b, 1)) for b in range(count - 1)]
    axes = ("core",) + BASIS
    low, high = store[:reach], store[rows - reach :]
    first = core == 0
    own_edge = lax.ppermute(jnp.where(first, high, low), axes, own_pairs)
    other_edge = lax.ppermute(jnp.where(first, low, high), axes, other_pairs)
    other = lax.ppermute(store, "core", SWAP)
    return store, other, own_edge, other_edge


def chip_half(second, state, owners, offsets, panels, dipole):
    nblk, terms = offsets.shape
    rows, width = panels[0].shape
    return pl.pallas_call(
        functools.partial(half_kernel, second),
        out_shape=jax.ShapeDtypeStruct((rows // 2, width), BF16),
        in_specs=[SMEM, SMEM, SMEM] + [VMEM] * 5,
        out_specs=VMEM,
        compiler_params=pltpu.CompilerParams(vmem_limit_bytes=12 << 20),
        cost_estimate=pl.CostEstimate(
            flops=nblk * terms * BS * BS * width, bytes_accessed=6 << 20, transcendentals=0
        ),
    )(state.reshape(1), owners, offsets, *panels, dipole)


def pick_kernel(owners_ref, pieces, seconds, copies, chunk):
    width = pieces.shape[2]
    for p in range(PANELS):
        owner = owners_ref[p]
        core, zlo, zhi, yhi = owner % 2, owner // 2 % 2, owner // 4 % SIZES["zhi"], owner // 16
        chip = (zlo * SIZES["yhi"] + yhi) * SIZES["zhi"] + zhi
        late = (core == 1) & owned(owners_ref, owner - 1)
        chunk[:, pl.ds(p * width, width)] = jnp.where(late, seconds[chip], pieces[chip])
    for i in range(copies.shape[0]):
        copies[i] = chunk[...]


def pick(owners, pieces, seconds):
    peers = lax.axis_size(GATHER)
    rows, width = pieces.shape[1:]
    return pl.pallas_call(
        pick_kernel,
        out_shape=jax.ShapeDtypeStruct((peers, rows, PANELS * width), BF16),
        in_specs=[SMEM, VMEM, VMEM],
        out_specs=VMEM,
        scratch_shapes=[pltpu.VMEM((rows, PANELS * width), BF16)],
        compiler_params=pltpu.CompilerParams(vmem_limit_bytes=8 << 20),
        cost_estimate=pl.CostEstimate(flops=0, bytes_accessed=1 << 20, transcendentals=0),
    )(owners, pieces, seconds)


def on_device(upper_coef, store, owners, dipole, offsets, lower_energy, upper_energy):
    core = lax.axis_index("core")
    state = lax.axis_index(STATE)
    width = store.shape[1]
    lowers = PANELS * width
    uppers = upper_coef.shape[1]
    zlo = lax.axis_index("zlo")
    quarter = upper_coef.shape[0] // 4

    def mine(flip_zlo, flip_core):
        start = ((core ^ flip_core) * 2 + (zlo ^ flip_zlo)) * quarter
        return lax.dynamic_slice_in_dim(upper_coef, start, quarter, 0)

    def from_peer(flip_zlo, flip_core):
        flip = 2 * flip_zlo + flip_core
        return lax.ppermute(mine(flip_zlo, flip_core), SHARED, [(i, i ^ flip) for i in range(4)])

    def beside(near, far):
        low = zlo == 0
        return jnp.concatenate([jnp.where(low, near, far), jnp.where(low, far, near)], 1)

    kinds = [from_peer(1, 1), from_peer(1, 0), from_peer(0, 1)]
    panels = chip_panels(store, core)
    half = chip_half(False, state, owners, offsets, panels, dipole)

    half, kinds[1] = lax.optimization_barrier((half, kinds[1]))

    def scatter(half):
        chips = lax.axis_size(CHIPS)
        return lax.all_to_all(half, CHIPS, 0, 0, tiled=True).reshape(chips, -1, width)

    pieces = scatter(half)
    pieces, kinds[2] = lax.optimization_barrier((pieces, kinds[2]))
    chips_of = owners // 2
    shared = jnp.sum((chips_of[:, None] == chips_of[None, :]).astype(jnp.int32)) > PANELS
    copies = lax.cond(
        shared,
        lambda: pick(
            owners, pieces, scatter(chip_half(True, state, owners, offsets, panels, dipole))
        ),
        lambda: pick(owners, pieces, pieces),
    )
    gathered = lax.all_to_all(copies.reshape(-1, lowers), GATHER, 0, 0, tiled=True)

    upper_other = beside(kinds[2], kinds[0])
    upper_own = beside(mine(0, 0), kinds[1])

    def share(rhs):
        return lax.dot_general(
            gathered, rhs, (((0,), (0,)), ((), ())), preferred_element_type=F32
        )

    received = lax.ppermute(share(upper_other).astype(BF16), "core", SWAP)
    kept, received = lax.optimization_barrier((share(upper_own), received))
    added = (kept + received.astype(F32)).astype(BF16)
    ranges = lax.axis_size(BASIS)
    sides = [added[:, :uppers], added[:, uppers:]]
    added = jnp.stack([side.reshape(ranges, -1, uppers) for side in sides], 1)
    added = added.reshape(2 * lowers, uppers)
    shares = lax.all_to_all(added, BASIS + ("zlo",), 0, 0, tiled=True)
    shares = shares.reshape(2 * ranges, -1, uppers)
    moments = jnp.sum(shares.astype(F32), axis=0)
    nu = upper_energy[None, :] - lower_energy[:, None]
    intensity = moments * moments * nu * jnp.exp(-lower_energy)[:, None] * (1.0 - jnp.exp(-nu))
    return moments, intensity


def solution(mesh):
    fine = Mesh(mesh.devices.reshape(tuple(SIZES.values())), tuple(SIZES))
    placed = (
        P(BASIS, STATE),
        P(BASIS, STATE),
        P(),
        P(BASIS, None, None, None),
        P(BASIS, None),
        P(BASIS),
        P(STATE),
    )
    return jax.shard_map(
        on_device,
        mesh=fine,
        in_specs=placed,
        out_specs=(P(BASIS, STATE), P(BASIS, STATE)),
        check_vma=False,
    )
```

```python
import functools

import jax
import jax.numpy as jnp
from jax import lax
from jax.experimental import pallas as pl
from jax.experimental.pallas import tpu as pltpu
from jax.sharding import Mesh
from jax.sharding import PartitionSpec as P

BS = 128
REACH = 2
PANELS = 4
BF16 = jnp.bfloat16
F32 = jnp.float32

SIZES = {"yhi": 4, "zhi": 4, "zlo": 2, "core": 2, "ylo": 2, "x": 4}
STATE = ("yhi", "zhi", "zlo", "core")
BASIS = ("ylo", "x")
SHARED = ("zlo", "core")
GATHER = ("yhi", "zhi")
CHIPS = ("zlo",) + GATHER
SWAP = [(0, 1), (1, 0)]

VMEM = pl.BlockSpec(memory_space=pltpu.VMEM)
SMEM = pl.BlockSpec(memory_space=pltpu.SMEM)


def owned(owners_ref, state):
    found = owners_ref[0] == state
    for p in range(1, PANELS):
        found = found | (owners_ref[p] == state)
    return found


def half_kernel(
    second, state_ref, owners_ref, offsets_ref, own, other, own_edge, other_edge, dipole, half
):
    nblk, terms = dipole.shape[0], dipole.shape[1]
    ncol = nblk // 2
    core = lax.rem(state_ref[0], 2)
    first = core * ncol
    if second:
        mine = core == 1
    else:
        mine = (core == 0) == owned(owners_ref, state_ref[0] - core)

    for j in range(ncol):
        column = first + j
        blocks = []
        for k in range(terms):
            block = column + offsets_ref[column, k]
            inside = (block >= 0) & (block < nblk)
            block_in = jnp.clip(block, 0, nblk - 1)
            source = pl.ds(pl.multiple_of(block_in * BS, BS), BS)
            rows = jnp.where(mine, own[source, :], other[source, :])
            if j < REACH or j >= ncol - REACH:
                place = jnp.where(block < 0, block + REACH, block - nblk)
                beyond = pl.ds(pl.multiple_of(jnp.clip(place, 0, REACH - 1) * BS, BS), BS)
                edge = jnp.where(mine, own_edge[beyond, :], other_edge[beyond, :])
                rows = jnp.where(inside, rows, edge)
            blocks.append(rows)
        half[pl.ds(j * BS, BS), :] = lax.dot_general(
            dipole[column].reshape(terms * BS, BS),
            jnp.concatenate(blocks, axis=0),
            (((0,), (0,)), ((), ())),
            preferred_element_type=F32,
        ).astype(BF16)


def chip_panels(store, core):
    rows = store.shape[0]
    reach = REACH * BS
    count = lax.axis_size(BASIS)

    def member(basis, kind):
        return basis + count * kind

    own_pairs = [(member(b, 0), member(b + 1, 0)) for b in range(count - 1)]
    own_pairs += [(member(b + 1, 1), member(b, 1)) for b in range(count - 1)]
    other_pairs = [(member(b, 1), member(b + 1, 0)) for b in range(count - 1)]
    other_pairs += [(member(b + 1, 0), member(b, 1)) for b in range(count - 1)]
    axes = ("core",) + BASIS
    low, high = store[:reach], store[rows - reach :]
    first = core == 0
    own_edge = lax.ppermute(jnp.where(first, high, low), axes, own_pairs)
    other_edge = lax.ppermute(jnp.where(first, low, high), axes, other_pairs)
    other = lax.ppermute(store, "core", SWAP)
    return store, other, own_edge, other_edge


def chip_half(second, state, owners, offsets, panels, dipole):
    nblk, terms = offsets.shape
    rows, width = panels[0].shape
    return pl.pallas_call(
        functools.partial(half_kernel, second),
        out_shape=jax.ShapeDtypeStruct((rows // 2, width), BF16),
        in_specs=[SMEM, SMEM, SMEM] + [VMEM] * 5,
        out_specs=VMEM,
        compiler_params=pltpu.CompilerParams(vmem_limit_bytes=12 << 20),
        cost_estimate=pl.CostEstimate(
            flops=nblk * terms * BS * BS * width, bytes_accessed=6 << 20, transcendentals=0
        ),
    )(state.reshape(1), owners, offsets, *panels, dipole)


def pick_kernel(owners_ref, pieces, seconds, copies, chunk):
    width = pieces.shape[2]
    for p in range(PANELS):
        owner = owners_ref[p]
        core, zlo, zhi, yhi = owner % 2, owner // 2 % 2, owner // 4 % SIZES["zhi"], owner // 16
        chip = (zlo * SIZES["yhi"] + yhi) * SIZES["zhi"] + zhi
        late = (core == 1) & owned(owners_ref, owner - 1)
        chunk[:, pl.ds(p * width, width)] = jnp.where(late, seconds[chip], pieces[chip])
    for i in range(copies.shape[0]):
        copies[i] = chunk[...]


def pick(owners, pieces, seconds):
    peers = lax.axis_size(GATHER)
    rows, width = pieces.shape[1:]
    return pl.pallas_call(
        pick_kernel,
        out_shape=jax.ShapeDtypeStruct((peers, rows, PANELS * width), BF16),
        in_specs=[SMEM, VMEM, VMEM],
        out_specs=VMEM,
        scratch_shapes=[pltpu.VMEM((rows, PANELS * width), BF16)],
        compiler_params=pltpu.CompilerParams(vmem_limit_bytes=8 << 20),
        cost_estimate=pl.CostEstimate(flops=0, bytes_accessed=1 << 20, transcendentals=0),
    )(owners, pieces, seconds)


def add_kernel(kept, received, added):
    ranges, sides, rows, width = added.shape
    for r in range(ranges):
        here = pl.ds(r * rows, rows)
        for side in range(sides):
            lanes = pl.ds(side * width, width)
            total = kept[here, lanes] + received[here, lanes].astype(F32)
            added[r, side] = total.astype(BF16)


def on_device(upper_coef, store, owners, dipole, offsets, lower_energy, upper_energy):
    core = lax.axis_index("core")
    state = lax.axis_index(STATE)
    width = store.shape[1]
    lowers = PANELS * width
    uppers = upper_coef.shape[1]
    zlo = lax.axis_index("zlo")
    quarter = upper_coef.shape[0] // 4

    def mine(rows, flip_zlo, flip_core):
        start = ((core ^ flip_core) * 2 + (zlo ^ flip_zlo)) * quarter
        return lax.dynamic_slice_in_dim(rows, start, quarter, 0)

    def from_peer(rows, flip_zlo, flip_core):
        flip = 2 * flip_zlo + flip_core
        piece = mine(rows, flip_zlo, flip_core)
        return lax.ppermute(piece, SHARED, [(i, i ^ flip) for i in range(4)])

    def beside(near, far):
        low = zlo == 0
        return jnp.concatenate([jnp.where(low, near, far), jnp.where(low, far, near)], 1)

    across_z = from_peer(upper_coef, 1, 0)
    panels = chip_panels(store, core)
    half = chip_half(False, state, owners, offsets, panels, dipole)

    half, across_z, later = lax.optimization_barrier((half, across_z, upper_coef))
    across_cores = from_peer(later, 0, 1)
    across_both = from_peer(later, 1, 1)

    def scatter(half):
        chips = lax.axis_size(CHIPS)
        return lax.all_to_all(half, CHIPS, 0, 0, tiled=True).reshape(chips, -1, width)

    pieces = scatter(half)
    pieces, across_cores = lax.optimization_barrier((pieces, across_cores))
    chips_of = owners // 2
    shared = jnp.sum((chips_of[:, None] == chips_of[None, :]).astype(jnp.int32)) > PANELS
    copies = lax.cond(
        shared,
        lambda: pick(
            owners, pieces, scatter(chip_half(True, state, owners, offsets, panels, dipole))
        ),
        lambda: pick(owners, pieces, pieces),
    )
    gathered = lax.all_to_all(copies.reshape(-1, lowers), GATHER, 0, 0, tiled=True)

    upper_other = beside(across_cores, across_both)
    upper_own = beside(mine(later, 0, 0), across_z)

    def share(rhs):
        return lax.dot_general(
            gathered, rhs, (((0,), (0,)), ((), ())), preferred_element_type=F32
        )

    received = lax.ppermute(share(upper_other).astype(BF16), "core", SWAP)
    kept = share(upper_own)
    ranges = lax.axis_size(BASIS)
    added = pl.pallas_call(
        add_kernel,
        out_shape=jax.ShapeDtypeStruct((ranges, 2, lowers // ranges, uppers), BF16),
        in_specs=[VMEM, VMEM],
        out_specs=VMEM,
        compiler_params=pltpu.CompilerParams(vmem_limit_bytes=8 << 20),
    )(kept, received).reshape(2 * lowers, uppers)
    shares = lax.all_to_all(added, BASIS + ("zlo",), 0, 0, tiled=True)
    shares = shares.reshape(2 * ranges, -1, uppers)
    moments = jnp.sum(shares.astype(F32), axis=0)
    nu = upper_energy[None, :] - lower_energy[:, None]
    intensity = moments * moments * nu * jnp.exp(-lower_energy)[:, None] * (1.0 - jnp.exp(-nu))
    return moments, intensity


def solution(mesh):
    fine = Mesh(mesh.devices.reshape(tuple(SIZES.values())), tuple(SIZES))
    placed = (
        P(BASIS, STATE),
        P(BASIS, STATE),
        P(),
        P(BASIS, None, None, None),
        P(BASIS, None),
        P(BASIS),
        P(STATE),
    )
    return jax.shard_map(
        on_device,
        mesh=fine,
        in_specs=placed,
        out_specs=(P(BASIS, STATE), P(BASIS, STATE)),
        check_vma=False,
    )
```

```python
import functools

import jax
import jax.numpy as jnp
from jax import lax
from jax.experimental import pallas as pl
from jax.experimental.pallas import tpu as pltpu
from jax.sharding import Mesh
from jax.sharding import PartitionSpec as P

BS = 128
REACH = 2
PANELS = 4
BF16 = jnp.bfloat16
F32 = jnp.float32

SIZES = {"yhi": 4, "zhi": 4, "zlo": 2, "core": 2, "ylo": 2, "x": 4}
STATE = ("yhi", "zhi", "zlo", "core")
BASIS = ("ylo", "x")
SHARED = ("zlo", "core")
GATHER = ("yhi", "zhi")
CHIPS = ("zlo",) + GATHER
SWAP = [(0, 1), (1, 0)]

VMEM = pl.BlockSpec(memory_space=pltpu.VMEM)
SMEM = pl.BlockSpec(memory_space=pltpu.SMEM)


def owned(owners_ref, state):
    found = owners_ref[0] == state
    for p in range(1, PANELS):
        found = found | (owners_ref[p] == state)
    return found


def half_kernel(
    second, state_ref, owners_ref, offsets_ref, own, other, own_edge, other_edge, dipole, half
):
    nblk, terms = dipole.shape[0], dipole.shape[1]
    ncol = nblk // 2
    core = lax.rem(state_ref[0], 2)
    first = core * ncol
    if second:
        mine = core == 1
    else:
        mine = (core == 0) == owned(owners_ref, state_ref[0] - core)

    for j in range(ncol):
        column = first + j
        blocks = []
        for k in range(terms):
            block = column + offsets_ref[column, k]
            inside = (block >= 0) & (block < nblk)
            block_in = jnp.clip(block, 0, nblk - 1)
            source = pl.ds(pl.multiple_of(block_in * BS, BS), BS)
            rows = jnp.where(mine, own[source, :], other[source, :])
            if j < REACH or j >= ncol - REACH:
                place = jnp.where(block < 0, block + REACH, block - nblk)
                beyond = pl.ds(pl.multiple_of(jnp.clip(place, 0, REACH - 1) * BS, BS), BS)
                edge = jnp.where(mine, own_edge[beyond, :], other_edge[beyond, :])
                rows = jnp.where(inside, rows, edge)
            blocks.append(rows)
        half[pl.ds(j * BS, BS), :] = lax.dot_general(
            dipole[column].reshape(terms * BS, BS),
            jnp.concatenate(blocks, axis=0),
            (((0,), (0,)), ((), ())),
            preferred_element_type=F32,
        ).astype(BF16)


def chip_panels(store, core):
    rows = store.shape[0]
    reach = REACH * BS
    count = lax.axis_size(BASIS)

    def member(basis, kind):
        return basis + count * kind

    own_pairs = [(member(b, 0), member(b + 1, 0)) for b in range(count - 1)]
    own_pairs += [(member(b + 1, 1), member(b, 1)) for b in range(count - 1)]
    other_pairs = [(member(b, 1), member(b + 1, 0)) for b in range(count - 1)]
    other_pairs += [(member(b + 1, 0), member(b, 1)) for b in range(count - 1)]
    axes = ("core",) + BASIS
    low, high = store[:reach], store[rows - reach :]
    first = core == 0
    own_edge = lax.ppermute(jnp.where(first, high, low), axes, own_pairs)
    other_edge = lax.ppermute(jnp.where(first, low, high), axes, other_pairs)
    other = lax.ppermute(store, "core", SWAP)
    return store, other, own_edge, other_edge


def chip_half(second, state, owners, offsets, panels, dipole):
    nblk, terms = offsets.shape
    rows, width = panels[0].shape
    return pl.pallas_call(
        functools.partial(half_kernel, second),
        out_shape=jax.ShapeDtypeStruct((rows // 2, width), BF16),
        in_specs=[SMEM, SMEM, SMEM] + [VMEM] * 5,
        out_specs=VMEM,
        compiler_params=pltpu.CompilerParams(vmem_limit_bytes=12 << 20),
        cost_estimate=pl.CostEstimate(
            flops=nblk * terms * BS * BS * width, bytes_accessed=6 << 20, transcendentals=0
        ),
    )(state.reshape(1), owners, offsets, *panels, dipole)


def pick_kernel(owners_ref, pieces, seconds, copies, chunk):
    width = pieces.shape[2]
    for p in range(PANELS):
        owner = owners_ref[p]
        core, zlo, zhi, yhi = owner % 2, owner // 2 % 2, owner // 4 % SIZES["zhi"], owner // 16
        chip = (zlo * SIZES["yhi"] + yhi) * SIZES["zhi"] + zhi
        late = (core == 1) & owned(owners_ref, owner - 1)
        chunk[:, pl.ds(p * width, width)] = jnp.where(late, seconds[chip], pieces[chip])
    for i in range(copies.shape[0]):
        copies[i] = chunk[...]


def pick(owners, pieces, seconds):
    peers = lax.axis_size(GATHER)
    rows, width = pieces.shape[1:]
    return pl.pallas_call(
        pick_kernel,
        out_shape=jax.ShapeDtypeStruct((peers, rows, PANELS * width), BF16),
        in_specs=[SMEM, VMEM, VMEM],
        out_specs=VMEM,
        scratch_shapes=[pltpu.VMEM((rows, PANELS * width), BF16)],
        compiler_params=pltpu.CompilerParams(vmem_limit_bytes=8 << 20),
        cost_estimate=pl.CostEstimate(flops=0, bytes_accessed=1 << 20, transcendentals=0),
    )(owners, pieces, seconds)


def add_kernel(kept, received, added):
    ranges, sides, rows, width = added.shape
    for r in range(ranges):
        here = pl.ds(r * rows, rows)
        for side in range(sides):
            lanes = pl.ds(side * width, width)
            total = kept[here, lanes] + received[here, lanes].astype(F32)
            added[r, side] = total.astype(BF16)


def on_device(upper_coef, store, owners, dipole, offsets, lower_energy, upper_energy):
    core = lax.axis_index("core")
    state = lax.axis_index(STATE)
    width = store.shape[1]
    lowers = PANELS * width
    uppers = upper_coef.shape[1]
    zlo = lax.axis_index("zlo")
    quarter = upper_coef.shape[0] // 4

    def mine(rows, flip_zlo, flip_core):
        start = ((core ^ flip_core) * 2 + (zlo ^ flip_zlo)) * quarter
        return lax.dynamic_slice_in_dim(rows, start, quarter, 0)

    def from_peer(rows, flip_zlo, flip_core):
        flip = 2 * flip_zlo + flip_core
        piece = mine(rows, flip_zlo, flip_core)
        return lax.ppermute(piece, SHARED, [(i, i ^ flip) for i in range(4)])

    def beside(near, far):
        low = zlo == 0
        return jnp.concatenate([jnp.where(low, near, far), jnp.where(low, far, near)], 1)

    across_z = from_peer(upper_coef, 1, 0)
    panels = chip_panels(store, core)
    half = chip_half(False, state, owners, offsets, panels, dipole)

    half, across_z, later = lax.optimization_barrier((half, across_z, upper_coef))
    across_both = from_peer(later, 1, 1)

    def scatter(half):
        chips = lax.axis_size(CHIPS)
        return lax.all_to_all(half, CHIPS, 0, 0, tiled=True).reshape(chips, -1, width)

    pieces = scatter(half)
    pieces, across_both, across_z, last = lax.optimization_barrier(
        (pieces, across_both, across_z, later)
    )
    across_cores = from_peer(last, 0, 1)
    chips_of = owners // 2
    shared = jnp.sum((chips_of[:, None] == chips_of[None, :]).astype(jnp.int32)) > PANELS
    copies = lax.cond(
        shared,
        lambda: pick(
            owners, pieces, scatter(chip_half(True, state, owners, offsets, panels, dipole))
        ),
        lambda: pick(owners, pieces, pieces),
    )
    gathered = lax.all_to_all(copies.reshape(-1, lowers), GATHER, 0, 0, tiled=True)

    upper_other = beside(across_cores, across_both)
    upper_own = beside(mine(last, 0, 0), across_z)

    def share(rhs):
        return lax.dot_general(
            gathered, rhs, (((0,), (0,)), ((), ())), preferred_element_type=F32
        )

    received = lax.ppermute(share(upper_other).astype(BF16), "core", SWAP)
    kept = share(upper_own)
    ranges = lax.axis_size(BASIS)
    added = pl.pallas_call(
        add_kernel,
        out_shape=jax.ShapeDtypeStruct((ranges, 2, lowers // ranges, uppers), BF16),
        in_specs=[VMEM, VMEM],
        out_specs=VMEM,
        compiler_params=pltpu.CompilerParams(vmem_limit_bytes=8 << 20),
    )(kept, received).reshape(2 * lowers, uppers)
    shares = lax.all_to_all(added, BASIS + ("zlo",), 0, 0, tiled=True)
    shares = shares.reshape(2 * ranges, -1, uppers)
    moments = jnp.sum(shares.astype(F32), axis=0)
    nu = upper_energy[None, :] - lower_energy[:, None]
    intensity = moments * moments * nu * jnp.exp(-lower_energy)[:, None] * (1.0 - jnp.exp(-nu))
    return moments, intensity


def solution(mesh):
    fine = Mesh(mesh.devices.reshape(tuple(SIZES.values())), tuple(SIZES))
    placed = (
        P(BASIS, STATE),
        P(BASIS, STATE),
        P(),
        P(BASIS, None, None, None),
        P(BASIS, None),
        P(BASIS),
        P(STATE),
    )
    return jax.shard_map(
        on_device,
        mesh=fine,
        in_specs=placed,
        out_specs=(P(BASIS, STATE), P(BASIS, STATE)),
        check_vma=False,
    )
```

```python
import functools

import jax
import jax.numpy as jnp
from jax import lax
from jax.experimental import pallas as pl
from jax.experimental.pallas import tpu as pltpu
from jax.sharding import Mesh
from jax.sharding import PartitionSpec as P

BS = 128
REACH = 2
PANELS = 4
BF16 = jnp.bfloat16
F32 = jnp.float32

SIZES = {"yhi": 4, "zhi": 4, "zlo": 2, "core": 2, "ylo": 2, "x": 4}
STATE = ("yhi", "zhi", "zlo", "core")
BASIS = ("ylo", "x")
SHARED = ("zlo", "core")
GATHER = ("yhi", "zhi")
CHIPS = ("zlo",) + GATHER
SWAP = [(0, 1), (1, 0)]

VMEM = pl.BlockSpec(memory_space=pltpu.VMEM)
SMEM = pl.BlockSpec(memory_space=pltpu.SMEM)


def owned(owners_ref, state):
    found = owners_ref[0] == state
    for p in range(1, PANELS):
        found = found | (owners_ref[p] == state)
    return found


def half_kernel(
    second, state_ref, owners_ref, offsets_ref, own, other, own_edge, other_edge, dipole, half
):
    nblk, terms = dipole.shape[0], dipole.shape[1]
    ncol = nblk // 2
    core = lax.rem(state_ref[0], 2)
    first = core * ncol
    if second:
        mine = core == 1
    else:
        mine = (core == 0) == owned(owners_ref, state_ref[0] - core)

    for j in range(ncol):
        column = first + j
        blocks = []
        for k in range(terms):
            block = column + offsets_ref[column, k]
            inside = (block >= 0) & (block < nblk)
            block_in = jnp.clip(block, 0, nblk - 1)
            source = pl.ds(pl.multiple_of(block_in * BS, BS), BS)
            rows = jnp.where(mine, own[source, :], other[source, :])
            if j < REACH or j >= ncol - REACH:
                place = jnp.where(block < 0, block + REACH, block - nblk)
                beyond = pl.ds(pl.multiple_of(jnp.clip(place, 0, REACH - 1) * BS, BS), BS)
                edge = jnp.where(mine, own_edge[beyond, :], other_edge[beyond, :])
                rows = jnp.where(inside, rows, edge)
            blocks.append(rows)
        half[pl.ds(j * BS, BS), :] = lax.dot_general(
            dipole[column].reshape(terms * BS, BS),
            jnp.concatenate(blocks, axis=0),
            (((0,), (0,)), ((), ())),
            preferred_element_type=F32,
        ).astype(BF16)


def chip_panels(store, core):
    rows = store.shape[0]
    reach = REACH * BS
    count = lax.axis_size(BASIS)

    def member(basis, kind):
        return basis + count * kind

    own_pairs = [(member(b, 0), member(b + 1, 0)) for b in range(count - 1)]
    own_pairs += [(member(b + 1, 1), member(b, 1)) for b in range(count - 1)]
    other_pairs = [(member(b, 1), member(b + 1, 0)) for b in range(count - 1)]
    other_pairs += [(member(b + 1, 0), member(b, 1)) for b in range(count - 1)]
    axes = ("core",) + BASIS
    low, high = store[:reach], store[rows - reach :]
    first = core == 0
    own_edge = lax.ppermute(jnp.where(first, high, low), axes, own_pairs)
    other_edge = lax.ppermute(jnp.where(first, low, high), axes, other_pairs)
    other = lax.ppermute(store, "core", SWAP)
    return store, other, own_edge, other_edge


def chip_half(second, state, owners, offsets, panels, dipole):
    nblk, terms = offsets.shape
    rows, width = panels[0].shape
    return pl.pallas_call(
        functools.partial(half_kernel, second),
        out_shape=jax.ShapeDtypeStruct((rows // 2, width), BF16),
        in_specs=[SMEM, SMEM, SMEM] + [VMEM] * 5,
        out_specs=VMEM,
        compiler_params=pltpu.CompilerParams(vmem_limit_bytes=12 << 20),
        cost_estimate=pl.CostEstimate(
            flops=nblk * terms * BS * BS * width, bytes_accessed=6 << 20, transcendentals=0
        ),
    )(state.reshape(1), owners, offsets, *panels, dipole)


def pick_kernel(owners_ref, pieces, seconds, copies, chunk):
    width = pieces.shape[2]
    for p in range(PANELS):
        owner = owners_ref[p]
        core, zlo, zhi, yhi = owner % 2, owner // 2 % 2, owner // 4 % SIZES["zhi"], owner // 16
        chip = (zlo * SIZES["yhi"] + yhi) * SIZES["zhi"] + zhi
        late = (core == 1) & owned(owners_ref, owner - 1)
        chunk[:, pl.ds(p * width, width)] = jnp.where(late, seconds[chip], pieces[chip])
    for i in range(copies.shape[0]):
        copies[i] = chunk[...]


def pick(owners, pieces, seconds):
    peers = lax.axis_size(GATHER)
    rows, width = pieces.shape[1:]
    return pl.pallas_call(
        pick_kernel,
        out_shape=jax.ShapeDtypeStruct((peers, rows, PANELS * width), BF16),
        in_specs=[SMEM, VMEM, VMEM],
        out_specs=VMEM,
        scratch_shapes=[pltpu.VMEM((rows, PANELS * width), BF16)],
        compiler_params=pltpu.CompilerParams(vmem_limit_bytes=8 << 20),
        cost_estimate=pl.CostEstimate(flops=0, bytes_accessed=1 << 20, transcendentals=0),
    )(owners, pieces, seconds)


def add_kernel(kept, received, added):
    ranges, sides, rows, width = added.shape
    for r in range(ranges):
        here = pl.ds(r * rows, rows)
        for side in range(sides):
            lanes = pl.ds(side * width, width)
            total = kept[here, lanes] + received[here, lanes].astype(F32)
            added[r, side] = total.astype(BF16)


def on_device(upper_coef, store, owners, dipole, offsets, lower_energy, upper_energy):
    core = lax.axis_index("core")
    state = lax.axis_index(STATE)
    width = store.shape[1]
    lowers = PANELS * width
    uppers = upper_coef.shape[1]
    zlo = lax.axis_index("zlo")
    quarter = upper_coef.shape[0] // 4

    def mine(rows, flip_zlo, flip_core):
        start = ((core ^ flip_core) * 2 + (zlo ^ flip_zlo)) * quarter
        return lax.dynamic_slice_in_dim(rows, start, quarter, 0)

    def swap(piece, flip_zlo, flip_core):
        flip = 2 * flip_zlo + flip_core
        return lax.ppermute(piece, SHARED, [(i, i ^ flip) for i in range(4)])

    def from_peer(rows, flip_zlo, flip_core):
        return swap(mine(rows, flip_zlo, flip_core), flip_zlo, flip_core)

    def beside(near, far):
        low = zlo == 0
        return jnp.concatenate([jnp.where(low, near, far), jnp.where(low, far, near)], 1)

    across_both = from_peer(upper_coef, 1, 1)
    panels = chip_panels(store, core)
    half = chip_half(False, state, owners, offsets, panels, dipole)

    half, across_both, later = lax.optimization_barrier((half, across_both, upper_coef))
    across_cores = from_peer(later, 0, 1)

    def scatter(half):
        chips = lax.axis_size(CHIPS)
        return lax.all_to_all(half, CHIPS, 0, 0, tiled=True).reshape(chips, -1, width)

    pieces = scatter(half)
    pieces, across_cores, sent = lax.optimization_barrier((pieces, across_cores, mine(later, 1, 0)))
    across_z = swap(sent, 1, 0)
    chips_of = owners // 2
    shared = jnp.sum((chips_of[:, None] == chips_of[None, :]).astype(jnp.int32)) > PANELS
    copies = lax.cond(
        shared,
        lambda: pick(
            owners, pieces, scatter(chip_half(True, state, owners, offsets, panels, dipole))
        ),
        lambda: pick(owners, pieces, pieces),
    )
    gathered = lax.all_to_all(copies.reshape(-1, lowers), GATHER, 0, 0, tiled=True)

    upper_other = beside(across_cores, across_both)
    upper_own = beside(mine(later, 0, 0), across_z)

    def share(rhs):
        return lax.dot_general(
            gathered, rhs, (((0,), (0,)), ((), ())), preferred_element_type=F32
        )

    received = lax.ppermute(share(upper_other).astype(BF16), "core", SWAP)
    kept = share(upper_own)
    ranges = lax.axis_size(BASIS)
    added = pl.pallas_call(
        add_kernel,
        out_shape=jax.ShapeDtypeStruct((ranges, 2, lowers // ranges, uppers), BF16),
        in_specs=[VMEM, VMEM],
        out_specs=VMEM,
        compiler_params=pltpu.CompilerParams(vmem_limit_bytes=8 << 20),
    )(kept, received).reshape(2 * lowers, uppers)
    shares = lax.all_to_all(added, BASIS + ("zlo",), 0, 0, tiled=True)
    shares = shares.reshape(2 * ranges, -1, uppers)
    moments = jnp.sum(shares.astype(F32), axis=0)
    nu = upper_energy[None, :] - lower_energy[:, None]
    intensity = moments * moments * nu * jnp.exp(-lower_energy)[:, None] * (1.0 - jnp.exp(-nu))
    return moments, intensity


def solution(mesh):
    fine = Mesh(mesh.devices.reshape(tuple(SIZES.values())), tuple(SIZES))
    placed = (
        P(BASIS, STATE),
        P(BASIS, STATE),
        P(),
        P(BASIS, None, None, None),
        P(BASIS, None),
        P(BASIS),
        P(STATE),
    )
    return jax.shard_map(
        on_device,
        mesh=fine,
        in_specs=placed,
        out_specs=(P(BASIS, STATE), P(BASIS, STATE)),
        check_vma=False,
    )
```

```python
import functools

import jax
import jax.numpy as jnp
from jax import lax
from jax.experimental import pallas as pl
from jax.experimental.pallas import tpu as pltpu
from jax.sharding import Mesh
from jax.sharding import PartitionSpec as P

BS = 128
REACH = 2
PANELS = 4
BF16 = jnp.bfloat16
F32 = jnp.float32

SIZES = {"yhi": 4, "zhi": 4, "zlo": 2, "core": 2, "ylo": 2, "x": 4}
STATE = ("yhi", "zhi", "zlo", "core")
BASIS = ("ylo", "x")
SHARED = ("zlo", "core")
GATHER = ("yhi", "zhi")
CHIPS = ("zlo",) + GATHER
SWAP = [(0, 1), (1, 0)]

VMEM = pl.BlockSpec(memory_space=pltpu.VMEM)
SMEM = pl.BlockSpec(memory_space=pltpu.SMEM)


def owned(owners_ref, state):
    found = owners_ref[0] == state
    for p in range(1, PANELS):
        found = found | (owners_ref[p] == state)
    return found


def half_kernel(
    second, state_ref, owners_ref, offsets_ref, own, other, own_edge, other_edge, dipole, half
):
    nblk, terms = dipole.shape[0], dipole.shape[1]
    ncol = nblk // 2
    core = lax.rem(state_ref[0], 2)
    first = core * ncol
    if second:
        mine = core == 1
    else:
        mine = (core == 0) == owned(owners_ref, state_ref[0] - core)

    for j in range(ncol):
        column = first + j
        blocks = []
        for k in range(terms):
            block = column + offsets_ref[column, k]
            inside = (block >= 0) & (block < nblk)
            block_in = jnp.clip(block, 0, nblk - 1)
            source = pl.ds(pl.multiple_of(block_in * BS, BS), BS)
            rows = jnp.where(mine, own[source, :], other[source, :])
            if j < REACH or j >= ncol - REACH:
                place = jnp.where(block < 0, block + REACH, block - nblk)
                beyond = pl.ds(pl.multiple_of(jnp.clip(place, 0, REACH - 1) * BS, BS), BS)
                edge = jnp.where(mine, own_edge[beyond, :], other_edge[beyond, :])
                rows = jnp.where(inside, rows, edge)
            blocks.append(rows)
        half[pl.ds(j * BS, BS), :] = lax.dot_general(
            dipole[column].reshape(terms * BS, BS),
            jnp.concatenate(blocks, axis=0),
            (((0,), (0,)), ((), ())),
            preferred_element_type=F32,
        ).astype(BF16)


def chip_panels(store, core):
    rows = store.shape[0]
    reach = REACH * BS
    count = lax.axis_size(BASIS)

    def member(basis, kind):
        return basis + count * kind

    own_pairs = [(member(b, 0), member(b + 1, 0)) for b in range(count - 1)]
    own_pairs += [(member(b + 1, 1), member(b, 1)) for b in range(count - 1)]
    other_pairs = [(member(b, 1), member(b + 1, 0)) for b in range(count - 1)]
    other_pairs += [(member(b + 1, 0), member(b, 1)) for b in range(count - 1)]
    axes = ("core",) + BASIS
    low, high = store[:reach], store[rows - reach :]
    first = core == 0
    own_edge = lax.ppermute(jnp.where(first, high, low), axes, own_pairs)
    other_edge = lax.ppermute(jnp.where(first, low, high), axes, other_pairs)
    other = lax.ppermute(store, "core", SWAP)
    return store, other, own_edge, other_edge


def chip_half(second, state, owners, offsets, panels, dipole):
    nblk, terms = offsets.shape
    rows, width = panels[0].shape
    return pl.pallas_call(
        functools.partial(half_kernel, second),
        out_shape=jax.ShapeDtypeStruct((rows // 2, width), BF16),
        in_specs=[SMEM, SMEM, SMEM] + [VMEM] * 5,
        out_specs=VMEM,
        compiler_params=pltpu.CompilerParams(vmem_limit_bytes=12 << 20),
        cost_estimate=pl.CostEstimate(
            flops=nblk * terms * BS * BS * width, bytes_accessed=6 << 20, transcendentals=0
        ),
    )(state.reshape(1), owners, offsets, *panels, dipole)


def pick_kernel(owners_ref, pieces, seconds, copies, chunk, sems):
    width = pieces.shape[2]
    for p in range(PANELS):
        owner = owners_ref[p]
        core, zlo, zhi, yhi = owner % 2, owner // 2 % 2, owner // 4 % SIZES["zhi"], owner // 16
        chip = (zlo * SIZES["yhi"] + yhi) * SIZES["zhi"] + zhi
        late = (core == 1) & owned(owners_ref, owner - 1)
        chunk[:, pl.ds(p * width, width)] = jnp.where(late, seconds[chip], pieces[chip])
    sends = [
        pltpu.make_async_copy(chunk, copies.at[i], sems.at[i]) for i in range(copies.shape[0])
    ]
    for send in sends:
        send.start()
    for send in sends:
        send.wait()


def pick(owners, pieces, seconds):
    peers = lax.axis_size(GATHER)
    rows, width = pieces.shape[1:]
    return pl.pallas_call(
        pick_kernel,
        out_shape=jax.ShapeDtypeStruct((peers, rows, PANELS * width), BF16),
        in_specs=[SMEM, VMEM, VMEM],
        out_specs=pl.BlockSpec(memory_space=pl.ANY),
        scratch_shapes=[
            pltpu.VMEM((rows, PANELS * width), BF16),
            pltpu.SemaphoreType.DMA((peers,)),
        ],
        compiler_params=pltpu.CompilerParams(vmem_limit_bytes=8 << 20),
        cost_estimate=pl.CostEstimate(flops=0, bytes_accessed=1 << 20, transcendentals=0),
    )(owners, pieces, seconds)


def add_kernel(kept, received, added):
    ranges, sides, rows, width = added.shape
    for r in range(ranges):
        here = pl.ds(r * rows, rows)
        for side in range(sides):
            lanes = pl.ds(side * width, width)
            total = kept[here, lanes] + received[here, lanes].astype(F32)
            added[r, side] = total.astype(BF16)


def on_device(upper_coef, store, owners, dipole, offsets, lower_energy, upper_energy):
    core = lax.axis_index("core")
    state = lax.axis_index(STATE)
    width = store.shape[1]
    lowers = PANELS * width
    uppers = upper_coef.shape[1]
    zlo = lax.axis_index("zlo")
    quarter = upper_coef.shape[0] // 4

    def mine(rows, flip_zlo, flip_core):
        start = ((core ^ flip_core) * 2 + (zlo ^ flip_zlo)) * quarter
        return lax.dynamic_slice_in_dim(rows, start, quarter, 0)

    def from_peer(rows, flip_zlo, flip_core):
        flip = 2 * flip_zlo + flip_core
        piece = mine(rows, flip_zlo, flip_core)
        return lax.ppermute(piece, SHARED, [(i, i ^ flip) for i in range(4)])

    def beside(near, far):
        low = zlo == 0
        return jnp.concatenate([jnp.where(low, near, far), jnp.where(low, far, near)], 1)

    across_z = from_peer(upper_coef, 1, 0)
    panels = chip_panels(store, core)
    half = chip_half(False, state, owners, offsets, panels, dipole)

    half, across_z, later = lax.optimization_barrier((half, across_z, upper_coef))
    across_cores = from_peer(later, 0, 1)
    across_both = from_peer(later, 1, 1)

    def scatter(half):
        chips = lax.axis_size(CHIPS)
        return lax.all_to_all(half, CHIPS, 0, 0, tiled=True).reshape(chips, -1, width)

    pieces = scatter(half)
    pieces, across_cores = lax.optimization_barrier((pieces, across_cores))
    chips_of = owners // 2
    shared = jnp.sum((chips_of[:, None] == chips_of[None, :]).astype(jnp.int32)) > PANELS
    copies = lax.cond(
        shared,
        lambda: pick(
            owners, pieces, scatter(chip_half(True, state, owners, offsets, panels, dipole))
        ),
        lambda: pick(owners, pieces, pieces),
    )
    gathered = lax.all_to_all(copies.reshape(-1, lowers), GATHER, 0, 0, tiled=True)

    upper_other = beside(across_cores, across_both)
    upper_own = beside(mine(later, 0, 0), across_z)

    def share(rhs):
        return lax.dot_general(
            gathered, rhs, (((0,), (0,)), ((), ())), preferred_element_type=F32
        )

    received = lax.ppermute(share(upper_other).astype(BF16), "core", SWAP)
    kept = share(upper_own)
    ranges = lax.axis_size(BASIS)
    added = pl.pallas_call(
        add_kernel,
        out_shape=jax.ShapeDtypeStruct((ranges, 2, lowers // ranges, uppers), BF16),
        in_specs=[VMEM, VMEM],
        out_specs=VMEM,
        compiler_params=pltpu.CompilerParams(vmem_limit_bytes=8 << 20),
    )(kept, received).reshape(2 * lowers, uppers)
    shares = lax.all_to_all(added, BASIS + ("zlo",), 0, 0, tiled=True)
    shares = shares.reshape(2 * ranges, -1, uppers)
    moments = jnp.sum(shares.astype(F32), axis=0)
    nu = upper_energy[None, :] - lower_energy[:, None]
    intensity = moments * moments * nu * jnp.exp(-lower_energy)[:, None] * (1.0 - jnp.exp(-nu))
    return moments, intensity


def solution(mesh):
    fine = Mesh(mesh.devices.reshape(tuple(SIZES.values())), tuple(SIZES))
    placed = (
        P(BASIS, STATE),
        P(BASIS, STATE),
        P(),
        P(BASIS, None, None, None),
        P(BASIS, None),
        P(BASIS),
        P(STATE),
    )
    return jax.shard_map(
        on_device,
        mesh=fine,
        in_specs=placed,
        out_specs=(P(BASIS, STATE), P(BASIS, STATE)),
        check_vma=False,
    )
```
